256 devices in a mesh: seg: 64 (over y, z, core), ch: 4 (over x).
Axes of the slice: x: 4, y: 4, z: 8, core: 2. Of those that a mesh axis runs over, the one named last changes fastest.
Arguments:
- voxels: bfloat16 [65536, 256], P('seg'), may hold values from -6 to 6
- neighbours: int32 [27, 65536], P(None, 'seg'), may hold values from -1 to 65535, as said below
- send_perm: int32 [64, 1024], P('seg'), may hold values from 0 to 1023, each once within a row
- send_counts: int32 [64, 64], replicated, may hold values from 0 to 32, as said below
- conv_weight: bfloat16 [27, 256, 256], P(None, None, 'ch'), may hold values from -0.078125 to 0.078125
- qkv_first: bfloat16 [256, 3, 256], P(None, None, 'ch'), may hold values from -3 to 3
- out_first: bfloat16 [256, 256], replicated, may hold values from -0.375 to 0.375
- qkv_second: bfloat16 [256, 3, 256], P(None, None, 'ch'), may hold values from -3 to 3
- out_second: bfloat16 [256, 256], replicated, may hold values from -0.375 to 0.375
Outputs:
- encoded: bfloat16 [65536, 256], P('seg', 'ch')
The draws below stay inside these ranges and needn't reach their ends.
Inputs may be any that keep to these rules, and one draw needn't show every extreme that they name: `neighbours`: -1 marks an absent neighbour; any other entry is a voxel within 128 positions of the entry's own voxel along the z-order curve, and the middle offset is the voxel itself. `send_counts`: each row sums to 1024; some Hilbert segment receives exactly 32 voxels from every z-order segment.
All inputs are finite; a program needn't handle non-finite values.
Results may differ from the reference program's by a relative error of at most 0.02.
Values may be sent and summed in bfloat16 or wider, within the bound.
No kernel may reach another device: no remote copies, remote signals or barrier semaphores. Data moves between devices by JAX's collectives and lax.ppermute only.
A program may use at most 64 MiB of HBM per device.

```python
import jax
import jax.numpy as jnp
from jax import lax

C = 256
HEADS = 16
HD = 16
PATCH = 1024
KOFF = 27
HALO = 128
V_DEV = 1024
SEGS = 64
VOXELS = 65536
CAP = 32
RMAX = 2048


def draw_neighbours(key, part):
    columns = jnp.arange(VOXELS, dtype=jnp.int32)
    offsets = jnp.arange(KOFF, dtype=jnp.int32)[:, None]
    jitter = jax.random.randint(jax.random.fold_in(key, 21), (KOFF, VOXELS), -HALO, HALO + 1)
    edge_rows = ((columns % 97 == 0) & (columns >= HALO))[None, :]
    jitter = jnp.where((offsets == 0) & edge_rows, -HALO, jitter)
    jitter = jnp.where(offsets == KOFF // 2, 0, jitter)
    present = jax.random.randint(jax.random.fold_in(key, 22), (KOFF, VOXELS), 0, 10) >= 4
    present = present | (offsets == KOFF // 2) | (offsets == 0) & edge_rows
    target = columns[None, :] + jitter
    inside = (target >= 0) & (target < VOXELS)
    return jnp.where(present & inside, target, -1).astype(jnp.int32)


def draw_send_counts(key, part):
    others = SEGS - 1
    chosen_count = V_DEV - CAP
    busiest = jax.random.randint(jax.random.fold_in(key, 31), (), 0, SEGS)
    source_keys = jax.random.split(jax.random.fold_in(key, 32), SEGS)
    groups = jnp.arange(others, dtype=jnp.int32)

    def one_source(source_key):
        shuffled = jax.random.permutation(source_key, others * CAP)
        picked = shuffled[:chosen_count] // CAP
        return jnp.sum((picked[:, None] == groups[None, :]).astype(jnp.int32), axis=0)
    spread = jax.vmap(one_source)(source_keys)
    targets = jnp.arange(SEGS, dtype=jnp.int32)
    shifted = jnp.clip(targets - (targets > busiest).astype(jnp.int32), 0, others - 1)
    counts = jnp.where((targets == busiest)[None, :], CAP, spread[:, shifted])
    return counts.astype(jnp.int32)


def qkv_table(key, seed_salt):
    drawn_table = jax.random.truncated_normal(jax.random.fold_in(key, seed_salt), -4.0, 4.0, (C, 3, C), jnp.float32) * C ** (-0.5)
    return drawn_table


def draw_qkv_first(key, part):
    return qkv_table(key, 41).astype(jnp.bfloat16)


def draw_qkv_second(key, part):
    return qkv_table(key, 51).astype(jnp.bfloat16)


def levels(own_key, shape, cuts, low, top_value):
    loudness = 1.0
    for dim, blocks in cuts:
        heights = jax.random.uniform(jax.random.fold_in(jax.random.fold_in(own_key, 6), dim), (blocks,), jnp.float32, low / len(cuts), top_value / len(cuts))
        loudness = loudness * jnp.repeat(jnp.exp(heights), shape[dim] // blocks).reshape((-1,) + (1,) * (len(shape) - 1 - dim))
    return loudness


def scatter_about(rng, shape, deviation, bound, shards=(), kind=jnp.bfloat16):
    drawn = deviation * jax.random.normal(rng, shape, jnp.float32)
    if shards:
        drawn = drawn * levels(rng, shape, shards, -0.22, 0.18)
    return jnp.clip(drawn, -bound, bound).astype(kind)


def setup_inputs(seed: int = 0) -> dict:
    key_of = jax.random.split(jax.random.key(seed), 10)
    return {
        "voxels": scatter_about(key_of[0], (VOXELS, C), 1.0, 6.0, ((0, 64),)),
        "neighbours": draw_neighbours(jax.random.fold_in(key_of[9], 71), 0),
        "send_perm": jax.vmap(lambda own: jax.random.permutation(own, V_DEV))(jax.random.split(key_of[2], SEGS)).reshape((SEGS, V_DEV)).astype(jnp.int32),
        "send_counts": draw_send_counts(jax.random.fold_in(key_of[9], 71), 0),
        "conv_weight": scatter_about(key_of[4], (KOFF, C, C), (KOFF * C) ** -0.5, 0.078125, ((2, 4),)),
        "qkv_first": draw_qkv_first(jax.random.fold_in(key_of[9], 71), 0),
        "out_first": scatter_about(key_of[6], (C, C), C ** -0.5, 0.375),
        "qkv_second": draw_qkv_second(jax.random.fold_in(key_of[9], 71), 0),
        "out_second": scatter_about(key_of[8], (C, C), C ** -0.5, 0.375),
    }


NORM_EPS = 1e-05
MASKED_SCORE = -1e+30

def layer_norm(rows_in):
    values32 = rows_in.astype(jnp.float32)
    centre = values32 - lax.optimization_barrier(jnp.mean(values32, axis=-1, keepdims=True))
    spread = lax.optimization_barrier(jnp.mean(centre * centre, axis=-1, keepdims=True))
    return (centre * lax.rsqrt(spread + NORM_EPS)).astype(jnp.bfloat16)

def project(normed, weight):
    product = jnp.dot(normed, weight.reshape(C, 3 * C), preferred_element_type=jnp.float32)
    return product.astype(jnp.bfloat16).reshape(normed.shape[0], 3, HEADS, HD)

def attend(qkv_rows, key_live):
    count_rows = qkv_rows.shape[0]
    grouped = qkv_rows.reshape(count_rows // PATCH, PATCH, 3, HEADS, HD)
    masks = key_live.reshape(count_rows // PATCH, PATCH)
    score_scale = HD ** (-0.5)

    def one_patch(packed_item):
        patch_rows, live_keys = packed_item
        queries = patch_rows[:, 0].astype(jnp.float32)
        key_rows = patch_rows[:, 1].astype(jnp.float32)
        value_rows = patch_rows[:, 2].astype(jnp.float32)
        scores = jnp.einsum('qhd,khd->hqk', queries, key_rows, precision=lax.Precision.HIGHEST) * score_scale
        scores = jnp.where(live_keys[None, None, :], scores, MASKED_SCORE)
        peak = lax.optimization_barrier(jnp.max(scores, axis=2, keepdims=True))
        powered = jnp.exp(scores - peak)
        normaliser = lax.optimization_barrier(jnp.sum(powered, axis=2))
        weights = powered.astype(jnp.bfloat16).astype(jnp.float32)
        blended = jnp.einsum('hqk,khd->qhd', weights, value_rows, precision=lax.Precision.HIGHEST)
        return (blended / jnp.transpose(normaliser)[:, :, None]).astype(jnp.bfloat16)
    return lax.map(one_patch, (grouped, masks)).reshape(count_rows, C)

def reference(voxels, neighbours, send_perm, send_counts, conv_weight, qkv_first, out_first, qkv_second, out_second):

    def conv_step(kernel_index, running):
        target = neighbours[kernel_index]
        picked = jnp.take(voxels, jnp.clip(target, 0, VOXELS - 1), axis=0)
        picked = jnp.where((target >= 0)[:, None], picked, jnp.zeros((), jnp.bfloat16))
        return running + jnp.dot(picked, conv_weight[kernel_index], preferred_element_type=jnp.float32)
    conv_sum = lax.fori_loop(0, KOFF, conv_step, jnp.zeros((VOXELS, C), jnp.float32))
    mixed_a = (voxels.astype(jnp.float32) + conv_sum).astype(jnp.bfloat16)
    qkv_a = project(layer_norm(mixed_a), qkv_first)
    heads_a = attend(qkv_a, jnp.ones((VOXELS,), bool))
    attn_one = jnp.dot(heads_a, out_first, preferred_element_type=jnp.float32)
    mixed_b = (mixed_a.astype(jnp.float32) + attn_one).astype(jnp.bfloat16)
    qkv_b = project(layer_norm(mixed_b), qkv_second)
    send_off = (jnp.cumsum(send_counts, axis=1) - send_counts).astype(jnp.int32)

    def one_owner(owner):
        column = lax.dynamic_index_in_dim(send_counts, owner, 1, keepdims=False)
        recv_off = (jnp.cumsum(column) - column).astype(jnp.int32)
        recv_end = recv_off + column
        slots = jnp.arange(RMAX, dtype=jnp.int32)
        source = lax.optimization_barrier(jnp.sum((recv_end[None, :] <= slots[:, None]).astype(jnp.int32), axis=1))
        source = jnp.minimum(source, SEGS - 1)
        within = slots - recv_off[source]
        live_keys = slots < jnp.sum(column)
        position = jnp.clip(send_off[source, owner] + within, 0, V_DEV - 1)
        global_row = source * V_DEV + send_perm[source, position]
        global_row = jnp.clip(global_row, 0, VOXELS - 1).astype(jnp.int32)
        rows_here = jnp.take(qkv_b, global_row, axis=0)
        heads_here = attend(rows_here, live_keys)
        return (heads_here, jnp.where(live_keys, global_row, VOXELS).astype(jnp.int32))
    outputs, homes = lax.map(one_owner, jnp.arange(SEGS, dtype=jnp.int32))
    heads_b = jnp.zeros((VOXELS + 1, C), jnp.bfloat16).at[homes.reshape(-1)].set(outputs.reshape(-1, C))[:VOXELS]
    attn_two = jnp.dot(heads_b, out_second, preferred_element_type=jnp.float32)
    return (mixed_b.astype(jnp.float32) + attn_two).astype(jnp.bfloat16)
```

```python
import jax
import jax.numpy as jnp
import numpy as np
from jax import lax
from jax.experimental import pallas as pl
from jax.experimental.pallas import tpu as pltpu
from jax.sharding import PartitionSpec as P

BF = jnp.bfloat16
F32 = jnp.float32
I32 = jnp.int32
HALO = 128
KOFF = 27
EPS = 1e-05
DEAD = -1e30
EXP_SCALE = float(16 ** (-0.5) * np.log2(np.e))
NT = (((1,), (1,)), ((), ()))
TN = (((0,), (0,)), ((), ()))
VM = pl.BlockSpec(memory_space=pltpu.VMEM)
SM = pl.BlockSpec(memory_space=pltpu.SMEM)
PARAMS = pltpu.CompilerParams(vmem_limit_bytes=50 << 20)


def iota(shape, dim):
    return lax.broadcasted_iota(I32, shape, dim)


def one_where(cond):
    return jnp.where(cond, 1.0, 0.0)


def norm_columns(x):
    centre = x - jnp.mean(x, axis=0, keepdims=True)
    spread = jnp.mean(centre * centre, axis=0, keepdims=True)
    return (centre * lax.rsqrt(spread + EPS)).astype(BF)


def place(pieces, ch, full_ref):
    size = pieces[0].shape[0]
    for j, piece in enumerate(pieces):
        owner = (ch + j) & 3
        full_ref[pl.ds(pl.multiple_of(owner * size, size), size), :] = piece[...]


def conv_kernel(ids, prev_ref, own_ref, next_ref, nb_ref, w_ref, out_ref, y_ref, acc_ref, nbs_ref):
    base = ids[0] * 1024 - HALO
    ch = ids[1]
    for b in range(8):
        nbs_ref[b * 32 : b * 32 + KOFF, :] = nb_ref[:, b * 128 : (b + 1) * 128]
    chosen = one_where(iota((64, 256), 1) == iota((64, 256), 0) + ch * 64).astype(BF)
    acc_ref[...] = lax.dot_general(chosen, own_ref[...], NT, preferred_element_type=F32)

    def transform(k, slot):
        w = w_ref[k]
        y_ref[slot, :, 0:128] = lax.dot_general(w, prev_ref[...], NT, preferred_element_type=F32)
        for j in range(4):
            y_ref[slot, :, 128 + j * 256 : 384 + j * 256] = lax.dot_general(
                w, own_ref[j * 256 : (j + 1) * 256], NT, preferred_element_type=F32
            )
        y_ref[slot, :, 1152:1280] = lax.dot_general(
            w, next_ref[...], NT, preferred_element_type=F32
        )

    def collect(k, slot):
        for b in range(8):
            r = nbs_ref[pl.ds(b * 32 + k, 8, stride=0), :] - (base + b * 128)
            there = nbs_ref[pl.ds(b * 32 + k, 8, stride=0), :] >= 0
            lane = r & 127
            first = r < 128
            second = r < 256
            for g in range(8):
                t = [
                    jnp.take_along_axis(
                        y_ref[slot, g * 8 : g * 8 + 8, (b + j) * 128 : (b + j + 1) * 128],
                        lane,
                        axis=1,
                        mode="promise_in_bounds",
                    )
                    for j in range(3)
                ]
                v = jnp.where(first, t[0], jnp.where(second, t[1], t[2]))
                acc_ref[g * 8 : g * 8 + 8, b * 128 : (b + 1) * 128] += jnp.where(there, v, 0.0)

    transform(0, 0)

    def body(i, carry):
        transform(2 * i + 1, 1)
        collect(2 * i, 0)
        transform(2 * i + 2, 0)
        collect(2 * i + 1, 1)
        return carry

    lax.fori_loop(0, KOFF // 2, body, 0)
    collect(KOFF - 1, 0)
    out_ref[...] = acc_ref[...].astype(BF)


def conv(ids, prev, own, nxt, nb, w):
    return pl.pallas_call(
        conv_kernel,
        name="conv",
        out_shape=jax.ShapeDtypeStruct((64, 1024), BF),
        in_specs=[SM] + [VM] * 5,
        out_specs=VM,
        scratch_shapes=[
            pltpu.VMEM((2, 64, 1280), F32),
            pltpu.VMEM((64, 1024), F32),
            pltpu.VMEM((256, 128), I32),
        ],
        compiler_params=PARAMS,
    )(ids, prev, own, nxt, nb, w)


def stage_heads(qkv, bias, q_ref, k_ref, v_ref):
    rows = qkv.shape[1]
    qkv16 = qkv.astype(BF)
    ones = jnp.ones((16, rows), BF)
    q_ref[...] = jnp.concatenate([qkv16[0:64], ones, jnp.zeros((48, rows), BF)], 0).T
    values = jnp.concatenate([qkv16[128:192], jnp.ones((64, rows), BF)], 0).T
    owner = (iota((1, 128), 1) & 63) >> 4
    k_ref[...] = jnp.zeros(k_ref.shape, BF)
    for h in range(4):
        k_ref[h, h * 16 : (h + 1) * 16, :] = qkv16[64 + h * 16 : 80 + h * 16]
        if bias is not None:
            k_ref[h, 64:80, :] = bias
        v_ref[h] = jnp.where(owner == h, values, jnp.zeros_like(values))


def attend(q_ref, k_ref, v_ref, patch, qb, block):
    start = patch * 1024
    if not isinstance(start, int):
        start = pl.multiple_of(start, 1024)
    rows = pl.ds(start + qb * block, block)
    keys = pl.ds(start, 1024)
    q = q_ref[rows, :]
    total = None
    for h in range(4):
        s = jnp.dot(q, k_ref[h, :, keys], preferred_element_type=F32)
        peak = jnp.max(s, axis=1, keepdims=True)
        p = jnp.exp2((s - peak) * EXP_SCALE).astype(BF)
        o = jnp.dot(p, v_ref[h, keys, :], preferred_element_type=F32)
        total = o if total is None else total + o
    return total / pltpu.roll(total, 64, 1)


def first_kernel(ids, x0, x1, x2, x3, w_ref, out_ref, full_ref, q_ref, k_ref, v_ref):
    place((x0, x1, x2, x3), ids[1], full_ref)
    normed = norm_columns(full_ref[...].astype(F32))
    qkv = jnp.dot(w_ref[...], normed, preferred_element_type=F32)
    stage_heads(qkv, None, q_ref, k_ref, v_ref)
    for qb in range(4):
        o = attend(q_ref, k_ref, v_ref, 0, qb, 256)
        out_ref[:, qb * 256 : (qb + 1) * 256] = o.T[:64].astype(BF)


def first(ids, pieces, w):
    return pl.pallas_call(
        first_kernel,
        name="first",
        out_shape=jax.ShapeDtypeStruct((64, 1024), BF),
        in_specs=[SM] + [VM] * 5,
        out_specs=VM,
        scratch_shapes=[
            pltpu.VMEM((256, 1024), BF),
            pltpu.VMEM((1024, 128), BF),
            pltpu.VMEM((4, 128, 1024), BF),
            pltpu.VMEM((4, 1024, 128), BF),
        ],
        compiler_params=PARAMS,
    )(ids, *pieces, w)


def pick_kernel(
    ids, x0, x1, x2, x3, h0, h1, h2, h3, wo_ref, perm_ref, counts_ref, send_ref, mine_ref, full_ref, heads_ref
):
    seg = ids[0]
    ch = ids[1]
    place((x0, x1, x2, x3), ch, full_ref)
    place((h0, h1, h2, h3), ch, heads_ref)
    mixed = full_ref[...].astype(F32) + lax.dot_general(
        wo_ref[...], heads_ref[...], TN, preferred_element_type=F32
    )
    mixed16 = mixed.astype(BF)
    full_ref[...] = mixed16
    mine_ref[...] = full_ref[pl.ds(pl.multiple_of(ch * 64, 64), 64), :]
    normed = norm_columns(mixed16.astype(F32))
    counts = counts_ref[...].astype(F32)
    row = jnp.sum(jnp.where(iota((64, 64), 0) == seg, counts, 0.0), axis=0, keepdims=True)
    slot = iota((512, 64), 0)
    before = jnp.where(iota((512, 64), 1) < (slot >> 3), row, 0.0)
    position = jnp.sum(before, axis=1, keepdims=True).astype(I32)
    position = position + ch * 8 + (iota((512, 1), 0) & 7)
    perm = perm_ref[...].astype(F32)
    hit = iota((512, 1024), 1) == position
    source = jnp.sum(jnp.where(hit, perm, 0.0), axis=1, keepdims=True).astype(I32)
    chosen = one_where(iota((512, 1024), 1) == source).astype(BF)
    rows = lax.dot_general(chosen, normed, NT, preferred_element_type=F32)
    send_ref[...] = rows.astype(BF).reshape(64, 8, 256)


def pick(ids, mixed, heads, wo, perm, counts):
    return pl.pallas_call(
        pick_kernel,
        name="pick",
        out_shape=(
            jax.ShapeDtypeStruct((64, 8, 256), BF),
            jax.ShapeDtypeStruct((64, 1024), BF),
        ),
        in_specs=[SM] + [VM] * 11,
        out_specs=(VM, VM),
        scratch_shapes=[pltpu.VMEM((256, 1024), BF), pltpu.VMEM((256, 1024), BF)],
        compiler_params=PARAMS,
    )(ids, *mixed, *heads, wo, perm, counts)


def second_kernel(
    ids, counts_sm, a0, a1, a2, a3, w_ref, out_ref, lo_ref, hi_ref, q_ref, k_ref, v_ref, o_ref
):
    seg = ids[0]
    ch = ids[1]
    lo_ref[...] = jnp.zeros(lo_ref.shape, F32)
    hi_ref[...] = jnp.zeros(hi_ref.shape, F32)

    def compact(s, off):
        tiles = [piece[s].astype(F32) for piece in (a0, a1, a2, a3)]
        for j, tile in enumerate(tiles):
            dst = pl.ds(off + ((ch + j) & 3) * 8, 8)
            lo_ref[dst, :] = tile[:, :128]
            hi_ref[dst, :] = tile[:, 128:]
        return off + counts_sm[s, seg]

    live = lax.fori_loop(0, 64, compact, 0)
    rows = jnp.concatenate([lo_ref[0:2048, :], hi_ref[0:2048, :]], 1).astype(BF)
    qkv = lax.dot_general(w_ref[...], rows, NT, preferred_element_type=F32)
    dead = (iota((16, 2048), 1) >= live) & (iota((16, 2048), 0) == 0)
    bias = jnp.where(dead, DEAD, 0.0).astype(BF)
    stage_heads(qkv, bias, q_ref, k_ref, v_ref)
    o_ref[2048:2080, :] = jnp.zeros((32, 128), F32)

    def block(i, carry):
        o = attend(q_ref, k_ref, v_ref, i >> 2, i & 3, 256)
        both = jnp.where(iota((1, 128), 1) < 64, o, pltpu.roll(o, 64, 1))
        o_ref[pl.ds(pl.multiple_of(i * 256, 256), 256), :] = both
        return carry

    lax.fori_loop(0, 8, block, 0)
    low = iota((16, 128), 1) < 64

    def give(s, off):
        top = o_ref[pl.ds(off, 16), :]
        end = o_ref[pl.ds(off + 16, 16), :]
        out_ref[s] = jnp.where(low, top, end).astype(BF)
        return off + counts_sm[s, seg]

    lax.fori_loop(0, 64, give, 0)


def second(ids, counts, arrived, w):
    return pl.pallas_call(
        second_kernel,
        name="second",
        out_shape=jax.ShapeDtypeStruct((64, 16, 128), BF),
        in_specs=[SM, SM] + [VM] * 5,
        out_specs=VM,
        scratch_shapes=[
            pltpu.VMEM((2080, 128), F32),
            pltpu.VMEM((2080, 128), F32),
            pltpu.VMEM((2048, 128), BF),
            pltpu.VMEM((4, 128, 2048), BF),
            pltpu.VMEM((4, 2048, 128), BF),
            pltpu.VMEM((2080, 128), F32),
        ],
        compiler_params=PARAMS,
    )(ids, counts, *arrived, w)


def home_kernel(ids, counts_sm, back_ref, perm_ref, out_ref, sorted_ref):
    seg = ids[0]

    def put(t, off):
        tile = back_ref[t].astype(F32)
        sorted_ref[pl.ds(off, 16), :] = tile
        sorted_ref[pl.ds(off + 16, 16), :] = pltpu.roll(tile, 64, 1)
        return off + counts_sm[seg, t]

    lax.fori_loop(0, 64, put, 0)
    chosen = one_where(iota((1024, 1024), 0) == perm_ref[...]).astype(BF)
    rows = jnp.dot(chosen, sorted_ref[0:1024, :].astype(BF), preferred_element_type=F32)
    out_ref[...] = rows.T[:64].astype(BF)


def home(ids, counts, back, perm):
    return pl.pallas_call(
        home_kernel,
        name="home",
        out_shape=jax.ShapeDtypeStruct((64, 1024), BF),
        in_specs=[SM, SM, VM, VM],
        out_specs=VM,
        scratch_shapes=[pltpu.VMEM((1056, 128), F32)],
        compiler_params=PARAMS,
    )(ids, counts, back, perm)


def last_kernel(ids, mine_ref, h0, h1, h2, h3, wo_ref, out_ref, heads_ref, all_ref):
    ch = ids[1]
    place((h0, h1, h2, h3), ch, heads_ref)
    all_ref[...] = lax.dot_general(
        wo_ref[...], heads_ref[...], TN, preferred_element_type=F32
    )
    own = all_ref[pl.ds(pl.multiple_of(ch * 64, 64), 64), :]
    out_ref[...] = (mine_ref[...].astype(F32) + own).astype(BF)


def last(ids, mine, heads, wo):
    return pl.pallas_call(
        last_kernel,
        name="last",
        out_shape=jax.ShapeDtypeStruct((64, 1024), BF),
        in_specs=[SM] + [VM] * 6,
        out_specs=VM,
        scratch_shapes=[pltpu.VMEM((256, 1024), BF), pltpu.VMEM((256, 1024), F32)],
        compiler_params=PARAMS,
    )(ids, mine, *heads, wo)


def spread(piece):
    def moved(step):
        return lax.ppermute(piece, "ch", [((i + step) % 4, i) for i in range(4)])

    return piece, moved(1), moved(2), moved(3)


def local(
    voxels, neighbours, send_perm, send_counts, conv_weight, qkv_first, out_first, qkv_second, out_second
):
    seg_count = lax.axis_size("seg")
    ids = jnp.stack([lax.axis_index("seg"), lax.axis_index("ch")]).astype(I32)
    up = [(i, i + 1) for i in range(seg_count - 1)]
    down = [(i + 1, i) for i in range(seg_count - 1)]
    prev = lax.ppermute(voxels[-HALO:], "seg", up)
    nxt = lax.ppermute(voxels[:HALO], "seg", down)
    conv_w = jnp.swapaxes(conv_weight, 1, 2)
    w_first = jnp.transpose(qkv_first, (1, 2, 0)).reshape(192, 256)
    w_second = jnp.transpose(qkv_second, (1, 2, 0)).reshape(192, 256)
    mixed_a = spread(conv(ids, prev, voxels, nxt, neighbours, conv_w))
    heads_a = spread(first(ids, mixed_a, w_first))
    outgoing, mine = pick(ids, mixed_a, heads_a, out_first, send_perm, send_counts)
    arrived = lax.all_to_all(outgoing, "seg", split_axis=0, concat_axis=0, tiled=True)
    going = second(ids, send_counts, spread(arrived), w_second)
    back = lax.all_to_all(going, "seg", split_axis=0, concat_axis=0, tiled=True)
    heads_b = spread(home(ids, send_counts, back, send_perm))
    return jnp.swapaxes(last(ids, mine, heads_b, out_second), 0, 1)


def solution(mesh):
    placed = (
        P("seg", None),
        P(None, "seg"),
        P("seg", None),
        P(),
        P(None, None, "ch"),
        P(None, None, "ch"),
        P(),
        P(None, None, "ch"),
        P(),
    )
    return jax.shard_map(
        local, mesh=mesh, in_specs=placed, out_specs=P("seg", "ch"), check_vma=False
    )
```

```python
import jax
import jax.numpy as jnp
import numpy as np
from jax import lax
from jax.experimental import pallas as pl
from jax.experimental.pallas import tpu as pltpu
from jax.sharding import PartitionSpec as P

BF = jnp.bfloat16
F32 = jnp.float32
I32 = jnp.int32
HALO = 128
KOFF = 27
EPS = 1e-05
DEAD = -1e30
EXP_SCALE = float(16 ** (-0.5) * np.log2(np.e))
NT = (((1,), (1,)), ((), ()))
TN = (((0,), (0,)), ((), ()))
VM = pl.BlockSpec(memory_space=pltpu.VMEM)
SM = pl.BlockSpec(memory_space=pltpu.SMEM)
PARAMS = pltpu.CompilerParams(vmem_limit_bytes=50 << 20)


def cost(us):
    return pl.CostEstimate(flops=int(us * 500e6), bytes_accessed=1 << 20, transcendentals=0)


def iota(shape, dim):
    return lax.broadcasted_iota(I32, shape, dim)


def one_where(cond):
    return jnp.where(cond, 1.0, 0.0)


def norm_columns(x):
    centre = x - jnp.mean(x, axis=0, keepdims=True)
    spread = jnp.mean(centre * centre, axis=0, keepdims=True)
    return (centre * lax.rsqrt(spread + EPS)).astype(BF)


def in_eights(step, start):
    def eight(i, carry):
        for j in range(8):
            carry = step(i * 8 + j, carry)
        return carry

    return lax.fori_loop(0, 8, eight, start)


def place(pieces, ch, full_ref):
    size = pieces[0].shape[0]
    for j, piece in enumerate(pieces):
        owner = (ch + j) & 3
        full_ref[pl.ds(pl.multiple_of(owner * size, size), size), :] = piece[...]


def conv_kernel(ids, own_ref, nb_ref, w_ref, out_ref, y_ref, nbs_ref):
    base = ids[0] * 1024 - HALO
    ch = ids[1]
    for b in range(8):
        nbs_ref[b * 32 : b * 32 + KOFF, :] = nb_ref[:, b * 128 : (b + 1) * 128]
    chosen = one_where(iota((64, 256), 1) == iota((64, 256), 0) + ch * 64).astype(BF)
    out_ref[...] = lax.dot_general(chosen, own_ref[...], NT, preferred_element_type=F32)

    def transform(k, slot):
        w = w_ref[k]
        for j in range(4):
            y_ref[slot, :, j * 256 : (j + 1) * 256] = lax.dot_general(
                w, own_ref[j * 256 : (j + 1) * 256], NT, preferred_element_type=F32
            )

    def collect(k, slot):
        for b in range(8):
            target = nbs_ref[pl.ds(b * 32 + k, 8, stride=0), :]
            r = target - (base + b * 128)
            there = target >= 0
            if b == 0:
                there = there & (r >= 128)
            if b == 7:
                there = there & (r < 256)
            lane = r & 127
            first = r < 128
            second = r < 256
            for g in range(8):
                t = [
                    jnp.take_along_axis(
                        y_ref[slot, g * 8 : g * 8 + 8, (b + j - 1) * 128 : (b + j) * 128],
                        lane,
                        axis=1,
                        mode="promise_in_bounds",
                    )
                    if 0 <= b + j - 1 < 8
                    else None
                    for j in range(3)
                ]
                v = t[1] if t[2] is None else t[2]
                if t[2] is not None:
                    v = jnp.where(second, t[1], t[2])
                if t[0] is not None:
                    v = jnp.where(first, t[0], v)
                out_ref[g * 8 : g * 8 + 8, b * 128 : (b + 1) * 128] += jnp.where(there, v, 0.0)

    transform(0, 0)

    def body(i, carry):
        transform(2 * i + 1, 1)
        collect(2 * i, 0)
        transform(2 * i + 2, 0)
        collect(2 * i + 1, 1)
        return carry

    lax.fori_loop(0, KOFF // 2, body, 0)
    collect(KOFF - 1, 0)


def conv(ids, own, nb, w):
    return pl.pallas_call(
        conv_kernel,
        name="conv",
        out_shape=jax.ShapeDtypeStruct((64, 1024), F32),
        in_specs=[SM] + [VM] * 3,
        out_specs=VM,
        scratch_shapes=[pltpu.VMEM((2, 64, 1024), F32), pltpu.VMEM((264, 128), I32)],
        compiler_params=PARAMS,
        cost_estimate=cost(8),
    )(ids, own, nb, w)


def edge_kernel(ids, prev_ref, next_ref, nb_ref, w_ref, sum_ref, out_ref, y_ref, acc_ref, nbs_ref):
    base = ids[0] * 1024 - HALO
    for i, b in enumerate((0, 7)):
        nbs_ref[i * 32 : i * 32 + KOFF, :] = nb_ref[:, b * 128 : (b + 1) * 128]
        acc_ref[:, i * 128 : (i + 1) * 128] = sum_ref[:, b * 128 : (b + 1) * 128]
    ends = jnp.concatenate([prev_ref[...], next_ref[...]], 0)
    for i in range(3):
        w = w_ref[i * 9 : (i + 1) * 9].reshape(576, 256)
        y = lax.dot_general(w, ends, NT, preferred_element_type=F32)
        y_ref[i * 9 : (i + 1) * 9] = y.reshape(9, 64, 256)

    def collect(k):
        for i, b in enumerate((0, 7)):
            target = nbs_ref[pl.ds(i * 32 + k, 8, stride=0), :]
            r = target - (base + b * 128)
            there = (target >= 0) & ((r < 128) if b == 0 else (r >= 256))
            lane = r & 127
            for g in range(8):
                at = (slice(g * 8, g * 8 + 8), slice(i * 128, (i + 1) * 128))
                v = jnp.take_along_axis(
                    y_ref[k, at[0], at[1]], lane, axis=1, mode="promise_in_bounds"
                )
                acc_ref[at] += jnp.where(there, v, 0.0)

    def body(i, carry):
        for j in range(3):
            collect(i * 3 + j)
        return carry

    lax.fori_loop(0, 9, body, 0)
    out_ref[:, 128:896] = sum_ref[:, 128:896].astype(BF)
    for i, b in enumerate((0, 7)):
        out_ref[:, b * 128 : (b + 1) * 128] = acc_ref[:, i * 128 : (i + 1) * 128].astype(BF)


def edge(ids, prev, nxt, nb, w, total):
    return pl.pallas_call(
        edge_kernel,
        name="edge",
        out_shape=jax.ShapeDtypeStruct((64, 1024), BF),
        in_specs=[SM] + [VM] * 5,
        out_specs=VM,
        scratch_shapes=[
            pltpu.VMEM((KOFF, 64, 256), F32),
            pltpu.VMEM((64, 256), F32),
            pltpu.VMEM((72, 128), I32),
        ],
        compiler_params=PARAMS,
        cost_estimate=cost(2),
    )(ids, prev, nxt, nb, w, total)


def prep_kernel(ids, after_ref, wo_ref, perm_ref, counts_ref, pick_ref, home_ref, own_ref):
    seg = ids[0]
    ch = ids[1]
    counts = counts_ref[...].astype(F32)
    row = jnp.sum(jnp.where(iota((64, 64), 0) == seg, counts, 0.0), axis=0, keepdims=True)
    slot = iota((512, 64), 0)
    before = jnp.where(iota((512, 64), 1) < (slot >> 3), row, 0.0)
    position = jnp.sum(before, axis=1, keepdims=True).astype(I32)
    position = position + ch * 8 + (iota((512, 1), 0) & 7)
    perm = perm_ref[...].astype(F32)
    hit = iota((512, 1024), 1) == position
    source = jnp.sum(jnp.where(hit, perm, 0.0), axis=1, keepdims=True).astype(I32)
    pick_ref[...] = one_where(iota((512, 1024), 1) == source).astype(BF)
    home_ref[...] = one_where(iota((1024, 1024), 0) == perm_ref[...]).astype(BF)
    chosen = one_where(iota((64, 256), 1) == iota((64, 256), 0) + ch * 64).astype(BF)
    own = lax.dot_general(chosen, wo_ref[...], NT, preferred_element_type=F32)
    own_ref[...] = own.astype(BF)


def prep(ids, after, wo, perm, counts):
    return pl.pallas_call(
        prep_kernel,
        name="prep",
        out_shape=(
            jax.ShapeDtypeStruct((512, 1024), BF),
            jax.ShapeDtypeStruct((1024, 1024), BF),
            jax.ShapeDtypeStruct((64, 256), BF),
        ),
        in_specs=[SM, pl.BlockSpec(memory_space=pl.ANY)] + [VM] * 3,
        out_specs=(VM, VM, VM),
        compiler_params=PARAMS,
        cost_estimate=cost(3),
    )(ids, after, wo, perm, counts)


def stage_heads(qkv, bias, q_ref, k_ref, v_ref):
    rows = qkv.shape[1]
    qkv16 = qkv.astype(BF)
    ones = jnp.ones((16, rows), BF)
    values = jnp.concatenate([qkv16[128:192], jnp.ones((64, rows), BF)], 0).T
    owner = (iota((1, 128), 1) & 63) >> 4
    for h in range(4):
        mine = qkv16[h * 16 : (h + 1) * 16]
        k_ref[h, 0:16, :] = qkv16[64 + h * 16 : 80 + h * 16]
        if bias is not None:
            mine = jnp.concatenate([mine, ones], 0)
            k_ref[h, 16:32, :] = bias
        q_ref[h] = mine.T
        v_ref[h] = jnp.where(owner == h, values, jnp.zeros_like(values))


def attend(q_ref, k_ref, v_ref, patch, qb, block):
    start = patch * 1024
    if not isinstance(start, int):
        start = pl.multiple_of(start, 1024)
    rows = pl.ds(start + qb * block, block)
    keys = pl.ds(start, 1024)
    def score(h):
        return jnp.dot(q_ref[h, rows, :], k_ref[h, :, keys], preferred_element_type=F32)

    def weigh(s):
        peak = jnp.max(s, axis=1, keepdims=True)
        return jnp.exp2((s - peak) * EXP_SCALE).astype(BF)

    ss = [score(h) for h in range(4)]
    ps = [weigh(s) for s in ss]
    total = jnp.dot(jnp.concatenate(ps, 1), jnp.concatenate([v_ref[h, keys, :] for h in range(4)], 0), preferred_element_type=F32)
    return total / pltpu.roll(total, 64, 1)


def first_kernel(ids, x0, x1, x2, x3, w_ref, out_ref, full_ref, q_ref, k_ref, v_ref):
    place((x0, x1, x2, x3), ids[1], full_ref)
    normed = norm_columns(full_ref[...].astype(F32))
    qkv = jnp.dot(w_ref[...], normed, preferred_element_type=F32)
    stage_heads(qkv, None, q_ref, k_ref, v_ref)
    for qb in range(4):
        o = attend(q_ref, k_ref, v_ref, 0, qb, 256)
        out_ref[:, qb * 256 : (qb + 1) * 256] = o.T[:64].astype(BF)


def first(ids, pieces, w):
    return pl.pallas_call(
        first_kernel,
        name="first",
        out_shape=jax.ShapeDtypeStruct((64, 1024), BF),
        in_specs=[SM] + [VM] * 5,
        out_specs=VM,
        scratch_shapes=[
            pltpu.VMEM((256, 1024), BF),
            pltpu.VMEM((4, 1024, 16), BF),
            pltpu.VMEM((4, 16, 1024), BF),
            pltpu.VMEM((4, 1024, 128), BF),
        ],
        compiler_params=PARAMS,
    )(ids, *pieces, w)


def pick_kernel(ids, x0, x1, x2, x3, h0, h1, h2, h3, wo_ref, chosen_ref, send_ref, mine_ref, full_ref, heads_ref):
    ch = ids[1]
    place((x0, x1, x2, x3), ch, full_ref)
    place((h0, h1, h2, h3), ch, heads_ref)
    mixed = full_ref[...].astype(F32) + lax.dot_general(
        wo_ref[...], heads_ref[...], TN, preferred_element_type=F32
    )
    mixed16 = mixed.astype(BF)
    full_ref[...] = mixed16
    mine_ref[...] = full_ref[pl.ds(pl.multiple_of(ch * 64, 64), 64), :]
    normed = norm_columns(mixed16.astype(F32))
    rows = lax.dot_general(chosen_ref[...], normed, NT, preferred_element_type=F32)
    send_ref[...] = rows.astype(BF).reshape(64, 8, 256)


def pick(ids, mixed, heads, wo, chosen):
    return pl.pallas_call(
        pick_kernel,
        name="pick",
        out_shape=(
            jax.ShapeDtypeStruct((64, 8, 256), BF),
            jax.ShapeDtypeStruct((64, 1024), BF),
        ),
        in_specs=[SM] + [VM] * 10,
        out_specs=(VM, VM),
        scratch_shapes=[pltpu.VMEM((256, 1024), BF), pltpu.VMEM((256, 1024), BF)],
        compiler_params=PARAMS,
        cost_estimate=cost(2),
    )(ids, *mixed, *heads, wo, chosen)


def second_kernel(
    ids, counts_sm, a0, a1, a2, a3, w_ref, out_ref, lo_ref, hi_ref, q_ref, k_ref, v_ref, o_ref
):
    seg = ids[0]
    ch = ids[1]
    lo_ref[...] = jnp.zeros(lo_ref.shape, F32)
    hi_ref[...] = jnp.zeros(hi_ref.shape, F32)

    def compact(s, off):
        tiles = [piece[s].astype(F32) for piece in (a0, a1, a2, a3)]
        for j, tile in enumerate(tiles):
            dst = pl.ds(off + ((ch + j) & 3) * 8, 8)
            lo_ref[dst, :] = tile[:, :128]
            hi_ref[dst, :] = tile[:, 128:]
        return off + counts_sm[s, seg]

    live = in_eights(compact, 0)
    rows = jnp.concatenate([lo_ref[0:2048, :], hi_ref[0:2048, :]], 1).astype(BF)
    qkv = lax.dot_general(w_ref[...], rows, NT, preferred_element_type=F32)
    dead = (iota((16, 2048), 1) >= live) & (iota((16, 2048), 0) == 0)
    bias = jnp.where(dead, DEAD, 0.0).astype(BF)
    stage_heads(qkv, bias, q_ref, k_ref, v_ref)
    o_ref[2048:2080, :] = jnp.zeros((32, 128), F32)

    def block(i, carry):
        o = attend(q_ref, k_ref, v_ref, i >> 2, i & 3, 256)
        both = jnp.where(iota((1, 128), 1) < 64, o, pltpu.roll(o, 64, 1))
        o_ref[pl.ds(pl.multiple_of(i * 256, 256), 256), :] = both
        return carry

    lax.fori_loop(0, 8, block, 0)
    low = iota((16, 128), 1) < 64

    def give(s, off):
        top = o_ref[pl.ds(off, 16), :]
        end = o_ref[pl.ds(off + 16, 16), :]
        out_ref[s] = jnp.where(low, top, end).astype(BF)
        return off + counts_sm[s, seg]

    in_eights(give, 0)


def second(ids, counts, arrived, w):
    return pl.pallas_call(
        second_kernel,
        name="second",
        out_shape=jax.ShapeDtypeStruct((64, 16, 128), BF),
        in_specs=[SM, SM] + [VM] * 5,
        out_specs=VM,
        scratch_shapes=[
            pltpu.VMEM((2080, 128), F32),
            pltpu.VMEM((2080, 128), F32),
            pltpu.VMEM((4, 2048, 32), BF),
            pltpu.VMEM((4, 32, 2048), BF),
            pltpu.VMEM((4, 2048, 128), BF),
            pltpu.VMEM((2080, 128), F32),
        ],
        compiler_params=PARAMS,
    )(ids, counts, *arrived, w)


def home_kernel(ids, counts_sm, back_ref, chosen_ref, out_ref, sorted_ref):
    seg = ids[0]

    def put(t, off):
        tile = back_ref[t].astype(F32)
        sorted_ref[pl.ds(off, 16), :] = tile
        sorted_ref[pl.ds(off + 16, 16), :] = pltpu.roll(tile, 64, 1)
        return off + counts_sm[seg, t]

    in_eights(put, 0)
    rows = jnp.dot(chosen_ref[...], sorted_ref[0:1024, :].astype(BF), preferred_element_type=F32)
    out_ref[...] = rows.T[:64].astype(BF)


def home(ids, counts, back, chosen):
    return pl.pallas_call(
        home_kernel,
        name="home",
        out_shape=jax.ShapeDtypeStruct((64, 1024), BF),
        in_specs=[SM, SM, VM, VM],
        out_specs=VM,
        scratch_shapes=[pltpu.VMEM((1056, 128), F32)],
        compiler_params=PARAMS,
    )(ids, counts, back, chosen)


def last_kernel(ids, mine_ref, h0, h1, h2, h3, wo_ref, out_ref, heads_ref):
    place((h0, h1, h2, h3), ids[1], heads_ref)
    own = jnp.dot(wo_ref[...], heads_ref[...], preferred_element_type=F32)
    out_ref[...] = (mine_ref[...].astype(F32) + own).astype(BF)


def last(ids, mine, heads, wo):
    return pl.pallas_call(
        last_kernel,
        name="last",
        out_shape=jax.ShapeDtypeStruct((64, 1024), BF),
        in_specs=[SM] + [VM] * 6,
        out_specs=VM,
        scratch_shapes=[pltpu.VMEM((256, 1024), BF)],
        compiler_params=PARAMS,
    )(ids, mine, *heads, wo)


def spread(piece):
    def moved(step):
        return lax.ppermute(piece, "ch", [((i + step) % 4, i) for i in range(4)])

    return piece, moved(1), moved(2), moved(3)


def local(
    voxels, neighbours, send_perm, send_counts, conv_weight, qkv_first, out_first, qkv_second, out_second
):
    seg_count = lax.axis_size("seg")
    ids = jnp.stack([lax.axis_index("seg"), lax.axis_index("ch")]).astype(I32)
    up = [(i, i + 1) for i in range(seg_count - 1)]
    down = [(i + 1, i) for i in range(seg_count - 1)]
    prev = lax.ppermute(voxels[-HALO:], "seg", up)
    nxt = lax.ppermute(voxels[:HALO], "seg", down)
    conv_w = jnp.swapaxes(conv_weight, 1, 2)
    w_first = jnp.transpose(qkv_first, (1, 2, 0)).reshape(192, 256)
    w_second = jnp.transpose(qkv_second, (1, 2, 0)).reshape(192, 256)
    own_sum = conv(ids, voxels, neighbours, conv_w)
    mixed_part = edge(ids, prev, nxt, neighbours, conv_w, own_sum)
    mixed_a = spread(mixed_part)
    pick_rows, home_rows, own_out = prep(ids, mixed_part, out_second, send_perm, send_counts)
    heads_a = spread(first(ids, mixed_a, w_first))
    outgoing, mine = pick(ids, mixed_a, heads_a, out_first, pick_rows)
    arrived = lax.all_to_all(outgoing, "seg", split_axis=0, concat_axis=0, tiled=True)
    going = second(ids, send_counts, spread(arrived), w_second)
    back = lax.all_to_all(going, "seg", split_axis=0, concat_axis=0, tiled=True)
    heads_b = spread(home(ids, send_counts, back, home_rows))
    return jnp.swapaxes(last(ids, mine, heads_b, own_out), 0, 1)


def solution(mesh):
    placed = (
        P("seg", None),
        P(None, "seg"),
        P("seg", None),
        P(),
        P(None, None, "ch"),
        P(None, None, "ch"),
        P(),
        P(None, None, "ch"),
        P(),
    )
    return jax.shard_map(
        local, mesh=mesh, in_specs=placed, out_specs=P("seg", "ch"), check_vma=False
    )
```

```python
import jax
import jax.numpy as jnp
import numpy as np
from jax import lax
from jax.experimental import pallas as pl
from jax.experimental.pallas import tpu as pltpu
from jax.sharding import PartitionSpec as P

BF = jnp.bfloat16
F32 = jnp.float32
I32 = jnp.int32
HALO = 128
KOFF = 27
EPS = 1e-05
DEAD = -1e30
EXP_SCALE = float(16 ** (-0.5) * np.log2(np.e))
SAFE_BOUND = float((40.0 * 4) ** 2)
TINY = 1e-30
NT = (((1,), (1,)), ((), ()))
TN = (((0,), (0,)), ((), ()))
VM = pl.BlockSpec(memory_space=pltpu.VMEM)
SM = pl.BlockSpec(memory_space=pltpu.SMEM)
PARAMS = pltpu.CompilerParams(vmem_limit_bytes=50 << 20)


def cost(us):
    return pl.CostEstimate(flops=int(us * 500e6), bytes_accessed=1 << 20, transcendentals=0)


def iota(shape, dim):
    return lax.broadcasted_iota(I32, shape, dim)


def one_where(cond):
    return jnp.where(cond, 1.0, 0.0)


def norm_columns(x):
    centre = x - jnp.mean(x, axis=0, keepdims=True)
    spread = jnp.mean(centre * centre, axis=0, keepdims=True)
    return (centre * lax.rsqrt(spread + EPS)).astype(BF)


def in_eights(step, start):
    def eight(i, carry):
        for j in range(8):
            carry = step(i * 8 + j, carry)
        return carry

    return lax.fori_loop(0, 8, eight, start)


def place(pieces, ch, full_ref):
    size = pieces[0].shape[0]
    for j, piece in enumerate(pieces):
        owner = (ch + j) & 3
        full_ref[pl.ds(pl.multiple_of(owner * size, size), size), :] = piece[...]


def conv_kernel(ids, own_ref, nb_ref, w_ref, out_ref, y_ref, nbs_ref):
    base = ids[0] * 1024 - HALO
    ch = ids[1]
    for b in range(8):
        nbs_ref[b * 32 : b * 32 + KOFF, :] = nb_ref[:, b * 128 : (b + 1) * 128]
    chosen = one_where(iota((64, 256), 1) == iota((64, 256), 0) + ch * 64).astype(BF)
    out_ref[...] = lax.dot_general(chosen, own_ref[...], NT, preferred_element_type=F32)

    def transform(k, slot):
        w = w_ref[k]
        for j in range(4):
            y_ref[slot, :, j * 256 : (j + 1) * 256] = lax.dot_general(
                w, own_ref[j * 256 : (j + 1) * 256], NT, preferred_element_type=F32
            )

    def collect(k, slot):
        for b in range(8):
            target = nbs_ref[pl.ds(b * 32 + k, 8, stride=0), :]
            r = target - (base + b * 128)
            there = target >= 0
            if b == 0:
                there = there & (r >= 128)
            if b == 7:
                there = there & (r < 256)
            lane = r & 127
            first = r < 128
            second = r < 256
            for g in range(8):
                t = [
                    jnp.take_along_axis(
                        y_ref[slot, g * 8 : g * 8 + 8, (b + j - 1) * 128 : (b + j) * 128],
                        lane,
                        axis=1,
                        mode="promise_in_bounds",
                    )
                    if 0 <= b + j - 1 < 8
                    else None
                    for j in range(3)
                ]
                v = t[1] if t[2] is None else t[2]
                if t[2] is not None:
                    v = jnp.where(second, t[1], t[2])
                if t[0] is not None:
                    v = jnp.where(first, t[0], v)
                out_ref[g * 8 : g * 8 + 8, b * 128 : (b + 1) * 128] += jnp.where(there, v, 0.0)

    transform(0, 0)

    def body(i, carry):
        transform(2 * i + 1, 1)
        collect(2 * i, 0)
        transform(2 * i + 2, 0)
        collect(2 * i + 1, 1)
        return carry

    lax.fori_loop(0, KOFF // 2, body, 0)
    collect(KOFF - 1, 0)


def conv(ids, own, nb, w):
    return pl.pallas_call(
        conv_kernel,
        name="conv",
        out_shape=jax.ShapeDtypeStruct((64, 1024), F32),
        in_specs=[SM] + [VM] * 3,
        out_specs=VM,
        scratch_shapes=[pltpu.VMEM((2, 64, 1024), F32), pltpu.VMEM((264, 128), I32)],
        compiler_params=PARAMS,
        cost_estimate=cost(8),
    )(ids, own, nb, w)


def edge_kernel(ids, prev_ref, next_ref, nb_ref, w_ref, sum_ref, out_ref, y_ref, acc_ref, nbs_ref):
    base = ids[0] * 1024 - HALO
    for i, b in enumerate((0, 7)):
        nbs_ref[i * 32 : i * 32 + KOFF, :] = nb_ref[:, b * 128 : (b + 1) * 128]
        acc_ref[:, i * 128 : (i + 1) * 128] = sum_ref[:, b * 128 : (b + 1) * 128]
    ends = jnp.concatenate([prev_ref[...], next_ref[...]], 0)
    for i in range(3):
        w = w_ref[i * 9 : (i + 1) * 9].reshape(576, 256)
        y = lax.dot_general(w, ends, NT, preferred_element_type=F32)
        y_ref[i * 9 : (i + 1) * 9] = y.reshape(9, 64, 256)

    def collect(k):
        for i, b in enumerate((0, 7)):
            target = nbs_ref[pl.ds(i * 32 + k, 8, stride=0), :]
            r = target - (base + b * 128)
            there = (target >= 0) & ((r < 128) if b == 0 else (r >= 256))
            lane = r & 127
            for g in range(8):
                at = (slice(g * 8, g * 8 + 8), slice(i * 128, (i + 1) * 128))
                v = jnp.take_along_axis(
                    y_ref[k, at[0], at[1]], lane, axis=1, mode="promise_in_bounds"
                )
                acc_ref[at] += jnp.where(there, v, 0.0)

    def body(i, carry):
        for j in range(3):
            collect(i * 3 + j)
        return carry

    lax.fori_loop(0, 9, body, 0)
    out_ref[:, 128:896] = sum_ref[:, 128:896].astype(BF)
    for i, b in enumerate((0, 7)):
        out_ref[:, b * 128 : (b + 1) * 128] = acc_ref[:, i * 128 : (i + 1) * 128].astype(BF)


def edge(ids, prev, nxt, nb, w, total):
    return pl.pallas_call(
        edge_kernel,
        name="edge",
        out_shape=jax.ShapeDtypeStruct((64, 1024), BF),
        in_specs=[SM] + [VM] * 5,
        out_specs=VM,
        scratch_shapes=[
            pltpu.VMEM((KOFF, 64, 256), F32),
            pltpu.VMEM((64, 256), F32),
            pltpu.VMEM((72, 128), I32),
        ],
        compiler_params=PARAMS,
        cost_estimate=cost(2),
    )(ids, prev, nxt, nb, w, total)


def prep_kernel(ids, after_ref, wo_ref, perm_ref, counts_ref, pick_ref, home_ref, own_ref):
    seg = ids[0]
    ch = ids[1]
    counts = counts_ref[...].astype(F32)
    row = jnp.sum(jnp.where(iota((64, 64), 0) == seg, counts, 0.0), axis=0, keepdims=True)
    slot = iota((512, 64), 0)
    before = jnp.where(iota((512, 64), 1) < (slot >> 3), row, 0.0)
    position = jnp.sum(before, axis=1, keepdims=True).astype(I32)
    position = position + ch * 8 + (iota((512, 1), 0) & 7)
    perm = perm_ref[...].astype(F32)
    hit = iota((512, 1024), 1) == position
    source = jnp.sum(jnp.where(hit, perm, 0.0), axis=1, keepdims=True).astype(I32)
    pick_ref[...] = one_where(iota((512, 1024), 1) == source).astype(BF)
    home_ref[...] = one_where(iota((1024, 1024), 0) == perm_ref[...]).astype(BF)
    chosen = one_where(iota((64, 256), 1) == iota((64, 256), 0) + ch * 64).astype(BF)
    own = lax.dot_general(chosen, wo_ref[...], NT, preferred_element_type=F32)
    own_ref[...] = own.astype(BF)


def prep(ids, after, wo, perm, counts):
    return pl.pallas_call(
        prep_kernel,
        name="prep",
        out_shape=(
            jax.ShapeDtypeStruct((512, 1024), BF),
            jax.ShapeDtypeStruct((1024, 1024), BF),
            jax.ShapeDtypeStruct((64, 256), BF),
        ),
        in_specs=[SM, pl.BlockSpec(memory_space=pl.ANY)] + [VM] * 3,
        out_specs=(VM, VM, VM),
        compiler_params=PARAMS,
        cost_estimate=cost(3),
    )(ids, after, wo, perm, counts)


def stage_heads(qkv, bias, q_ref, k_ref, v_ref):
    rows = qkv.shape[1]
    qkv16 = qkv.astype(BF)
    ones = jnp.ones((16, rows), BF)
    for h in range(4):
        key = qkv16[64 + h * 16 : 80 + h * 16]
        q_ref[h, 0:16, :] = qkv16[h * 16 : (h + 1) * 16]
        if bias is not None:
            key = jnp.concatenate([key, bias], 0)
            q_ref[h, 16:32, :] = ones
        k_ref[h] = key.T
        v_ref[h, 0:16, :] = qkv16[128 + h * 16 : 144 + h * 16]
        v_ref[h, 16:32, :] = ones
    square = qkv16[0:128].astype(F32)
    square = square * square
    longest = [
        jnp.max(jnp.sum(square[i * 16 : (i + 1) * 16], axis=0, keepdims=True)) for i in range(8)
    ]
    bound = longest[0] * longest[4]
    for h in range(1, 4):
        bound = jnp.maximum(bound, longest[h] * longest[4 + h])
    return bound <= SAFE_BOUND


def attend(q_ref, k_ref, v_ref, out_ref, h, keys, cols, shifted):
    s = jnp.dot(k_ref[h, keys, :], q_ref[h, :, cols], preferred_element_type=F32)
    if shifted:
        s = s - jnp.max(s, axis=0, keepdims=True)
    p = jnp.exp2(s * EXP_SCALE).astype(BF)
    o = jnp.dot(v_ref[h, :, keys], p, preferred_element_type=F32)
    o = o[:16] / jnp.maximum(o[16:17], TINY)
    at = h * 16 if isinstance(h, int) else pl.multiple_of(h * 16, 16)
    out_ref[pl.ds(at, 16), cols] = o.astype(out_ref.dtype)


def attend_all(safe, q_ref, k_ref, v_ref, out_ref, patches, block):
    def window(start, size, aligned):
        return pl.ds(start if isinstance(start, int) else pl.multiple_of(start, aligned), size)

    @pl.when(safe)
    def plain():
        def patch(i, carry):
            keys = window(i * 1024, 1024, 1024)
            for qb in range(1024 // block):
                cols = window(i * 1024 + qb * block, block, block)
                for h in range(4):
                    attend(q_ref, k_ref, v_ref, out_ref, h, keys, cols, False)
            return carry

        if patches == 1:
            patch(0, 0)
        else:
            lax.fori_loop(0, patches, patch, 0)

    @pl.when(jnp.logical_not(safe))
    def with_peak():
        def piece(i, carry):
            keys = window((i >> 3) * 1024, 1024, 1024)
            cols = window((i >> 3) * 1024 + (i & 1) * 512, 512, 512)
            attend(q_ref, k_ref, v_ref, out_ref, (i >> 1) & 3, keys, cols, True)
            return carry

        lax.fori_loop(0, patches * 8, piece, 0)


def first_kernel(ids, x0, x1, x2, x3, w_ref, out_ref, full_ref, q_ref, k_ref, v_ref):
    place((x0, x1, x2, x3), ids[1], full_ref)
    normed = norm_columns(full_ref[...].astype(F32))
    qkv = jnp.dot(w_ref[...], normed, preferred_element_type=F32)
    safe = stage_heads(qkv, None, q_ref, k_ref, v_ref)
    attend_all(safe, q_ref, k_ref, v_ref, out_ref, 1, 512)


def first(ids, pieces, w):
    return pl.pallas_call(
        first_kernel,
        name="first",
        out_shape=jax.ShapeDtypeStruct((64, 1024), BF),
        in_specs=[SM] + [VM] * 5,
        out_specs=VM,
        scratch_shapes=[
            pltpu.VMEM((256, 1024), BF),
            pltpu.VMEM((4, 16, 1024), BF),
            pltpu.VMEM((4, 1024, 16), BF),
            pltpu.VMEM((4, 32, 1024), BF),
        ],
        compiler_params=PARAMS,
    )(ids, *pieces, w)


def pick_kernel(ids, x0, x1, x2, x3, h0, h1, h2, h3, wo_ref, chosen_ref, send_ref, mine_ref, full_ref, heads_ref):
    ch = ids[1]
    place((x0, x1, x2, x3), ch, full_ref)
    place((h0, h1, h2, h3), ch, heads_ref)
    mixed = full_ref[...].astype(F32) + lax.dot_general(
        wo_ref[...], heads_ref[...], TN, preferred_element_type=F32
    )
    mixed16 = mixed.astype(BF)
    full_ref[...] = mixed16
    mine_ref[...] = full_ref[pl.ds(pl.multiple_of(ch * 64, 64), 64), :]
    normed = norm_columns(mixed16.astype(F32))
    rows = lax.dot_general(chosen_ref[...], normed, NT, preferred_element_type=F32)
    send_ref[...] = rows.astype(BF).reshape(64, 8, 256)


def pick(ids, mixed, heads, wo, chosen):
    return pl.pallas_call(
        pick_kernel,
        name="pick",
        out_shape=(
            jax.ShapeDtypeStruct((64, 8, 256), BF),
            jax.ShapeDtypeStruct((64, 1024), BF),
        ),
        in_specs=[SM] + [VM] * 10,
        out_specs=(VM, VM),
        scratch_shapes=[pltpu.VMEM((256, 1024), BF), pltpu.VMEM((256, 1024), BF)],
        compiler_params=PARAMS,
        cost_estimate=cost(2),
    )(ids, *mixed, *heads, wo, chosen)


def second_kernel(
    ids, counts_sm, a0, a1, a2, a3, w_ref, out_ref, lo_ref, hi_ref, q_ref, k_ref, v_ref, o_ref, heads_ref
):
    seg = ids[0]
    ch = ids[1]
    lo_ref[...] = jnp.zeros(lo_ref.shape, F32)
    hi_ref[...] = jnp.zeros(hi_ref.shape, F32)

    def compact(s, off):
        tiles = [piece[s].astype(F32) for piece in (a0, a1, a2, a3)]
        for j, tile in enumerate(tiles):
            dst = pl.ds(off + ((ch + j) & 3) * 8, 8)
            lo_ref[dst, :] = tile[:, :128]
            hi_ref[dst, :] = tile[:, 128:]
        return off + counts_sm[s, seg]

    live = in_eights(compact, 0)
    rows = jnp.concatenate([lo_ref[0:2048, :], hi_ref[0:2048, :]], 1).astype(BF)
    qkv = lax.dot_general(w_ref[...], rows, NT, preferred_element_type=F32)
    dead = (iota((16, 2048), 1) >= live) & (iota((16, 2048), 0) == 0)
    bias = jnp.where(dead, DEAD, 0.0).astype(BF)
    safe = stage_heads(qkv, bias, q_ref, k_ref, v_ref)
    o_ref[2048:2080, :] = jnp.zeros((32, 128), F32)

    attend_all(safe, q_ref, k_ref, v_ref, heads_ref, 2, 1024)
    for i in range(2):
        rows = slice(i * 1024, (i + 1) * 1024)
        o = heads_ref[:, rows]
        o_ref[rows, :] = jnp.concatenate([o, o], 0).T
    low = iota((16, 128), 1) < 64

    def give(s, off):
        top = o_ref[pl.ds(off, 16), :]
        end = o_ref[pl.ds(off + 16, 16), :]
        out_ref[s] = jnp.where(low, top, end).astype(BF)
        return off + counts_sm[s, seg]

    in_eights(give, 0)


def second(ids, counts, arrived, w):
    return pl.pallas_call(
        second_kernel,
        name="second",
        out_shape=jax.ShapeDtypeStruct((64, 16, 128), BF),
        in_specs=[SM, SM] + [VM] * 5,
        out_specs=VM,
        scratch_shapes=[
            pltpu.VMEM((2080, 128), F32),
            pltpu.VMEM((2080, 128), F32),
            pltpu.VMEM((4, 32, 2048), BF),
            pltpu.VMEM((4, 2048, 32), BF),
            pltpu.VMEM((4, 32, 2048), BF),
            pltpu.VMEM((2080, 128), F32),
            pltpu.VMEM((64, 2048), F32),
        ],
        compiler_params=PARAMS,
    )(ids, counts, *arrived, w)


def home_kernel(ids, counts_sm, back_ref, chosen_ref, out_ref, sorted_ref):
    seg = ids[0]

    def put(t, off):
        tile = back_ref[t].astype(F32)
        sorted_ref[pl.ds(off, 16), :] = tile
        sorted_ref[pl.ds(off + 16, 16), :] = pltpu.roll(tile, 64, 1)
        return off + counts_sm[seg, t]

    in_eights(put, 0)
    rows = jnp.dot(chosen_ref[...], sorted_ref[0:1024, :].astype(BF), preferred_element_type=F32)
    out_ref[...] = rows.T[:64].astype(BF)


def home(ids, counts, back, chosen):
    return pl.pallas_call(
        home_kernel,
        name="home",
        out_shape=jax.ShapeDtypeStruct((64, 1024), BF),
        in_specs=[SM, SM, VM, VM],
        out_specs=VM,
        scratch_shapes=[pltpu.VMEM((1056, 128), F32)],
        compiler_params=PARAMS,
    )(ids, counts, back, chosen)


def last_kernel(ids, mine_ref, h0, h1, h2, h3, wo_ref, out_ref, heads_ref):
    place((h0, h1, h2, h3), ids[1], heads_ref)
    own = jnp.dot(wo_ref[...], heads_ref[...], preferred_element_type=F32)
    out_ref[...] = (mine_ref[...].astype(F32) + own).astype(BF)


def last(ids, mine, heads, wo):
    return pl.pallas_call(
        last_kernel,
        name="last",
        out_shape=jax.ShapeDtypeStruct((64, 1024), BF),
        in_specs=[SM] + [VM] * 6,
        out_specs=VM,
        scratch_shapes=[pltpu.VMEM((256, 1024), BF)],
        compiler_params=PARAMS,
    )(ids, mine, *heads, wo)


def spread(piece):
    def moved(step):
        return lax.ppermute(piece, "ch", [((i + step) % 4, i) for i in range(4)])

    return piece, moved(1), moved(2), moved(3)


def local(
    voxels, neighbours, send_perm, send_counts, conv_weight, qkv_first, out_first, qkv_second, out_second
):
    seg_count = lax.axis_size("seg")
    ids = jnp.stack([lax.axis_index("seg"), lax.axis_index("ch")]).astype(I32)
    up = [(i, i + 1) for i in range(seg_count - 1)]
    down = [(i + 1, i) for i in range(seg_count - 1)]
    prev = lax.ppermute(voxels[-HALO:], "seg", up)
    nxt = lax.ppermute(voxels[:HALO], "seg", down)
    conv_w = jnp.swapaxes(conv_weight, 1, 2)
    w_first = jnp.transpose(qkv_first, (1, 2, 0)).reshape(192, 256)
    w_second = jnp.transpose(qkv_second, (1, 2, 0)).reshape(192, 256)
    own_sum = conv(ids, voxels, neighbours, conv_w)
    mixed_part = edge(ids, prev, nxt, neighbours, conv_w, own_sum)
    mixed_a = spread(mixed_part)
    pick_rows, home_rows, own_out = prep(ids, mixed_part, out_second, send_perm, send_counts)
    heads_a = spread(first(ids, mixed_a, w_first))
    outgoing, mine = pick(ids, mixed_a, heads_a, out_first, pick_rows)
    arrived = lax.all_to_all(outgoing, "seg", split_axis=0, concat_axis=0, tiled=True)
    going = second(ids, send_counts, spread(arrived), w_second)
    back = lax.all_to_all(going, "seg", split_axis=0, concat_axis=0, tiled=True)
    heads_b = spread(home(ids, send_counts, back, home_rows))
    return jnp.swapaxes(last(ids, mine, heads_b, own_out), 0, 1)


def solution(mesh):
    placed = (
        P("seg", None),
        P(None, "seg"),
        P("seg", None),
        P(),
        P(None, None, "ch"),
        P(None, None, "ch"),
        P(),
        P(None, None, "ch"),
        P(),
    )
    return jax.shard_map(
        local, mesh=mesh, in_specs=placed, out_specs=P("seg", "ch"), check_vma=False
    )
```

```python
import jax
import jax.numpy as jnp
import numpy as np
from jax import lax
from jax.experimental import pallas as pl
from jax.experimental.pallas import tpu as pltpu
from jax.sharding import PartitionSpec as P

BF = jnp.bfloat16
F32 = jnp.float32
I32 = jnp.int32
HALO = 128
KOFF = 27
EPS = 1e-05
DEAD = -1e30
EXP_SCALE = float(16 ** (-0.5) * np.log2(np.e))
SAFE_BOUND = float((40.0 * 4) ** 2)
TINY = 1e-30
NT = (((1,), (1,)), ((), ()))
TN = (((0,), (0,)), ((), ()))
VM = pl.BlockSpec(memory_space=pltpu.VMEM)
SM = pl.BlockSpec(memory_space=pltpu.SMEM)
PARAMS = pltpu.CompilerParams(vmem_limit_bytes=50 << 20)


def cost(us):
    return pl.CostEstimate(flops=int(us * 500e6), bytes_accessed=1 << 20, transcendentals=0)


def iota(shape, dim):
    return lax.broadcasted_iota(I32, shape, dim)


def one_where(cond):
    return jnp.where(cond, 1.0, 0.0)


def norm_columns(x):
    centre = x - jnp.mean(x, axis=0, keepdims=True)
    spread = jnp.mean(centre * centre, axis=0, keepdims=True)
    return (centre * lax.rsqrt(spread + EPS)).astype(BF)


def in_eights(step, start):
    def eight(i, carry):
        for j in range(8):
            carry = step(i * 8 + j, carry)
        return carry

    return lax.fori_loop(0, 8, eight, start)


def place(pieces, ch, full_ref):
    size = pieces[0].shape[0]
    for j, piece in enumerate(pieces):
        owner = (ch + j) & 3
        full_ref[pl.ds(pl.multiple_of(owner * size, size), size), :] = piece[...]


def conv_kernel(
    ids, own_hbm, nb_hbm, w_hbm, out_ref, own_ref, nb_ref, w_ref, y_ref, nbs_ref, sems
):
    base = ids[0] * 1024 - HALO
    ch = ids[1]
    pairs = ((nb_hbm, nb_ref), (own_hbm, own_ref), (w_hbm, w_ref))
    copies = [pltpu.make_async_copy(a, b, sems.at[i]) for i, (a, b) in enumerate(pairs)]
    for copy in copies:
        copy.start()
    copies[0].wait()
    for b in range(8):
        nbs_ref[b * 32 : b * 32 + KOFF, :] = nb_ref[:, b * 128 : (b + 1) * 128]
    chosen = one_where(iota((64, 256), 1) == iota((64, 256), 0) + ch * 64).astype(BF)
    copies[1].wait()
    out_ref[...] = lax.dot_general(chosen, own_ref[...], NT, preferred_element_type=F32)
    copies[2].wait()

    def transform(k, slot):
        w = w_ref[k]
        for j in range(4):
            y_ref[slot, :, j * 256 : (j + 1) * 256] = lax.dot_general(
                w, own_ref[j * 256 : (j + 1) * 256], NT, preferred_element_type=F32
            )

    def collect(k, slot):
        for b in range(8):
            target = nbs_ref[pl.ds(b * 32 + k, 8, stride=0), :]
            r = target - (base + b * 128)
            there = target >= 0
            if b == 0:
                there = there & (r >= 128)
            if b == 7:
                there = there & (r < 256)
            lane = r & 127
            first = r < 128
            second = r < 256
            for g in range(8):
                t = [
                    jnp.take_along_axis(
                        y_ref[slot, g * 8 : g * 8 + 8, (b + j - 1) * 128 : (b + j) * 128],
                        lane,
                        axis=1,
                        mode="promise_in_bounds",
                    )
                    if 0 <= b + j - 1 < 8
                    else None
                    for j in range(3)
                ]
                v = t[1] if t[2] is None else t[2]
                if t[2] is not None:
                    v = jnp.where(second, t[1], t[2])
                if t[0] is not None:
                    v = jnp.where(first, t[0], v)
                out_ref[g * 8 : g * 8 + 8, b * 128 : (b + 1) * 128] += jnp.where(there, v, 0.0)

    transform(0, 0)

    def body(i, carry):
        transform(2 * i + 1, 1)
        collect(2 * i, 0)
        transform(2 * i + 2, 0)
        collect(2 * i + 1, 1)
        return carry

    lax.fori_loop(0, KOFF // 2, body, 0)
    collect(KOFF - 1, 0)


def conv(ids, own, nb, w):
    stay = [pltpu.with_memory_space_constraint(x, pltpu.HBM) for x in (own, nb, w)]
    return pl.pallas_call(
        conv_kernel,
        name="conv",
        out_shape=jax.ShapeDtypeStruct((64, 1024), F32),
        in_specs=[SM] + [pl.BlockSpec(memory_space=pltpu.HBM)] * 3,
        out_specs=VM,
        scratch_shapes=[
            pltpu.VMEM((1024, 256), BF),
            pltpu.VMEM((KOFF, 1024), I32),
            pltpu.VMEM((KOFF, 64, 256), BF),
            pltpu.VMEM((2, 64, 1024), F32),
            pltpu.VMEM((264, 128), I32),
            pltpu.SemaphoreType.DMA((3,)),
        ],
        compiler_params=PARAMS,
        cost_estimate=cost(8),
    )(ids, *stay)


def edge_kernel(ids, prev_ref, next_ref, nb_ref, w_ref, sum_ref, out_ref, y_ref, acc_ref, nbs_ref):
    base = ids[0] * 1024 - HALO
    for i, b in enumerate((0, 7)):
        nbs_ref[i * 32 : i * 32 + KOFF, :] = nb_ref[:, b * 128 : (b + 1) * 128]
        acc_ref[:, i * 128 : (i + 1) * 128] = sum_ref[:, b * 128 : (b + 1) * 128]
    ends = jnp.concatenate([prev_ref[...], next_ref[...]], 0)
    for i in range(3):
        w = w_ref[i * 9 : (i + 1) * 9].reshape(576, 256)
        y = lax.dot_general(w, ends, NT, preferred_element_type=F32)
        y_ref[i * 9 : (i + 1) * 9] = y.reshape(9, 64, 256)

    def collect(k):
        for i, b in enumerate((0, 7)):
            target = nbs_ref[pl.ds(i * 32 + k, 8, stride=0), :]
            r = target - (base + b * 128)
            there = (target >= 0) & ((r < 128) if b == 0 else (r >= 256))
            lane = r & 127
            for g in range(8):
                at = (slice(g * 8, g * 8 + 8), slice(i * 128, (i + 1) * 128))
                v = jnp.take_along_axis(
                    y_ref[k, at[0], at[1]], lane, axis=1, mode="promise_in_bounds"
                )
                acc_ref[at] += jnp.where(there, v, 0.0)

    def body(i, carry):
        for j in range(3):
            collect(i * 3 + j)
        return carry

    lax.fori_loop(0, 9, body, 0)
    out_ref[:, 128:896] = sum_ref[:, 128:896].astype(BF)
    for i, b in enumerate((0, 7)):
        out_ref[:, b * 128 : (b + 1) * 128] = acc_ref[:, i * 128 : (i + 1) * 128].astype(BF)


def edge(ids, prev, nxt, nb, w, total):
    return pl.pallas_call(
        edge_kernel,
        name="edge",
        out_shape=jax.ShapeDtypeStruct((64, 1024), BF),
        in_specs=[SM] + [VM] * 5,
        out_specs=VM,
        scratch_shapes=[
            pltpu.VMEM((KOFF, 64, 256), F32),
            pltpu.VMEM((64, 256), F32),
            pltpu.VMEM((72, 128), I32),
        ],
        compiler_params=PARAMS,
        cost_estimate=cost(2),
    )(ids, prev, nxt, nb, w, total)


def prep_kernel(ids, after_ref, wo_ref, perm_ref, counts_ref, pick_ref, home_ref, own_ref):
    seg = ids[0]
    ch = ids[1]
    counts = counts_ref[...].astype(F32)
    row = jnp.sum(jnp.where(iota((64, 64), 0) == seg, counts, 0.0), axis=0, keepdims=True)
    slot = iota((512, 64), 0)
    before = jnp.where(iota((512, 64), 1) < (slot >> 3), row, 0.0)
    position = jnp.sum(before, axis=1, keepdims=True).astype(I32)
    position = position + ch * 8 + (iota((512, 1), 0) & 7)
    perm = perm_ref[...].astype(F32)
    hit = iota((512, 1024), 1) == position
    source = jnp.sum(jnp.where(hit, perm, 0.0), axis=1, keepdims=True).astype(I32)
    pick_ref[...] = one_where(iota((512, 1024), 1) == source).astype(BF)
    home_ref[...] = one_where(iota((1024, 1024), 0) == perm_ref[...]).astype(BF)
    chosen = one_where(iota((64, 256), 1) == iota((64, 256), 0) + ch * 64).astype(BF)
    own = lax.dot_general(chosen, wo_ref[...], NT, preferred_element_type=F32)
    own_ref[...] = own.astype(BF)


def prep(ids, after, wo, perm, counts):
    return pl.pallas_call(
        prep_kernel,
        name="prep",
        out_shape=(
            jax.ShapeDtypeStruct((512, 1024), BF),
            jax.ShapeDtypeStruct((1024, 1024), BF),
            jax.ShapeDtypeStruct((64, 256), BF),
        ),
        in_specs=[SM, pl.BlockSpec(memory_space=pl.ANY)] + [VM] * 3,
        out_specs=(VM, VM, VM),
        compiler_params=PARAMS,
        cost_estimate=cost(3),
    )(ids, after, wo, perm, counts)


def stage_heads(qkv, bias, q_ref, k_ref, v_ref):
    rows = qkv.shape[1]
    qkv16 = qkv.astype(BF)
    ones = jnp.ones((16, rows), BF)
    for h in range(4):
        key = qkv16[64 + h * 16 : 80 + h * 16]
        q_ref[h, 0:16, :] = qkv16[h * 16 : (h + 1) * 16]
        if bias is not None:
            key = jnp.concatenate([key, bias], 0)
            q_ref[h, 16:32, :] = ones
        k_ref[h] = key.T
        v_ref[h, 0:16, :] = qkv16[128 + h * 16 : 144 + h * 16]
        v_ref[h, 16:32, :] = ones
    square = qkv16[0:128].astype(F32)
    square = square * square
    longest = [
        jnp.max(jnp.sum(square[i * 16 : (i + 1) * 16], axis=0, keepdims=True)) for i in range(8)
    ]
    bound = longest[0] * longest[4]
    for h in range(1, 4):
        bound = jnp.maximum(bound, longest[h] * longest[4 + h])
    return bound <= SAFE_BOUND


def attend(q_ref, k_ref, v_ref, out_ref, h, keys, cols, shifted):
    s = jnp.dot(k_ref[h, keys, :], q_ref[h, :, cols], preferred_element_type=F32)
    if shifted:
        s = s - jnp.max(s, axis=0, keepdims=True)
    p = jnp.exp2(s * EXP_SCALE).astype(BF)
    o = jnp.dot(v_ref[h, :, keys], p, preferred_element_type=F32)
    o = o[:16] / jnp.maximum(o[16:17], TINY)
    at = h * 16 if isinstance(h, int) else pl.multiple_of(h * 16, 16)
    out_ref[pl.ds(at, 16), cols] = o.astype(out_ref.dtype)


def attend_all(safe, q_ref, k_ref, v_ref, out_ref, patches, block):
    def window(start, size, aligned):
        return pl.ds(start if isinstance(start, int) else pl.multiple_of(start, aligned), size)

    @pl.when(safe)
    def plain():
        def patch(i, carry):
            keys = window(i * 1024, 1024, 1024)
            for qb in range(1024 // block):
                cols = window(i * 1024 + qb * block, block, block)
                for h in range(4):
                    attend(q_ref, k_ref, v_ref, out_ref, h, keys, cols, False)
            return carry

        if patches == 1:
            patch(0, 0)
        else:
            lax.fori_loop(0, patches, patch, 0)

    @pl.when(jnp.logical_not(safe))
    def with_peak():
        def piece(i, carry):
            keys = window((i >> 3) * 1024, 1024, 1024)
            cols = window((i >> 3) * 1024 + (i & 1) * 512, 512, 512)
            attend(q_ref, k_ref, v_ref, out_ref, (i >> 1) & 3, keys, cols, True)
            return carry

        lax.fori_loop(0, patches * 8, piece, 0)


def first_kernel(ids, x0, x1, x2, x3, w_ref, out_ref, full_ref, q_ref, k_ref, v_ref):
    place((x0, x1, x2, x3), ids[1], full_ref)
    normed = norm_columns(full_ref[...].astype(F32))
    qkv = jnp.dot(w_ref[...], normed, preferred_element_type=F32)
    safe = stage_heads(qkv, None, q_ref, k_ref, v_ref)
    attend_all(safe, q_ref, k_ref, v_ref, out_ref, 1, 512)


def first(ids, pieces, w):
    return pl.pallas_call(
        first_kernel,
        name="first",
        out_shape=jax.ShapeDtypeStruct((64, 1024), BF),
        in_specs=[SM] + [VM] * 5,
        out_specs=VM,
        scratch_shapes=[
            pltpu.VMEM((256, 1024), BF),
            pltpu.VMEM((4, 16, 1024), BF),
            pltpu.VMEM((4, 1024, 16), BF),
            pltpu.VMEM((4, 32, 1024), BF),
        ],
        compiler_params=PARAMS,
    )(ids, *pieces, w)


def pick_kernel(ids, x0, x1, x2, x3, h0, h1, h2, h3, wo_ref, chosen_ref, send_ref, mine_ref, full_ref, heads_ref):
    ch = ids[1]
    place((x0, x1, x2, x3), ch, full_ref)
    place((h0, h1, h2, h3), ch, heads_ref)
    mixed = full_ref[...].astype(F32) + lax.dot_general(
        wo_ref[...], heads_ref[...], TN, preferred_element_type=F32
    )
    mixed16 = mixed.astype(BF)
    full_ref[...] = mixed16
    mine_ref[...] = full_ref[pl.ds(pl.multiple_of(ch * 64, 64), 64), :]
    normed = norm_columns(mixed16.astype(F32))
    rows = lax.dot_general(chosen_ref[...], normed, NT, preferred_element_type=F32)
    send_ref[...] = rows.astype(BF).reshape(64, 8, 256)


def pick(ids, mixed, heads, wo, chosen):
    return pl.pallas_call(
        pick_kernel,
        name="pick",
        out_shape=(
            jax.ShapeDtypeStruct((64, 8, 256), BF),
            jax.ShapeDtypeStruct((64, 1024), BF),
        ),
        in_specs=[SM] + [VM] * 10,
        out_specs=(VM, VM),
        scratch_shapes=[pltpu.VMEM((256, 1024), BF), pltpu.VMEM((256, 1024), BF)],
        compiler_params=PARAMS,
        cost_estimate=cost(2),
    )(ids, *mixed, *heads, wo, chosen)


def second_kernel(
    ids, counts_sm, a0, a1, a2, a3, w_ref, out_ref, lo_ref, hi_ref, q_ref, k_ref, v_ref, o_ref, heads_ref
):
    seg = ids[0]
    ch = ids[1]
    lo_ref[...] = jnp.zeros(lo_ref.shape, F32)
    hi_ref[...] = jnp.zeros(hi_ref.shape, F32)

    def compact(s, off):
        tiles = [piece[s].astype(F32) for piece in (a0, a1, a2, a3)]
        for j, tile in enumerate(tiles):
            dst = pl.ds(off + ((ch + j) & 3) * 8, 8)
            lo_ref[dst, :] = tile[:, :128]
            hi_ref[dst, :] = tile[:, 128:]
        return off + counts_sm[s, seg]

    live = in_eights(compact, 0)
    rows = jnp.concatenate([lo_ref[0:2048, :], hi_ref[0:2048, :]], 1).astype(BF)
    qkv = lax.dot_general(w_ref[...], rows, NT, preferred_element_type=F32)
    dead = (iota((16, 2048), 1) >= live) & (iota((16, 2048), 0) == 0)
    bias = jnp.where(dead, DEAD, 0.0).astype(BF)
    safe = stage_heads(qkv, bias, q_ref, k_ref, v_ref)
    o_ref[2048:2080, :] = jnp.zeros((32, 128), F32)

    attend_all(safe, q_ref, k_ref, v_ref, heads_ref, 2, 1024)
    for i in range(2):
        rows = slice(i * 1024, (i + 1) * 1024)
        o = heads_ref[:, rows]
        o_ref[rows, :] = jnp.concatenate([o, o], 0).T
    low = iota((16, 128), 1) < 64

    def give(s, off):
        top = o_ref[pl.ds(off, 16), :]
        end = o_ref[pl.ds(off + 16, 16), :]
        out_ref[s] = jnp.where(low, top, end).astype(BF)
        return off + counts_sm[s, seg]

    in_eights(give, 0)


def second(ids, counts, arrived, w):
    return pl.pallas_call(
        second_kernel,
        name="second",
        out_shape=jax.ShapeDtypeStruct((64, 16, 128), BF),
        in_specs=[SM, SM] + [VM] * 5,
        out_specs=VM,
        scratch_shapes=[
            pltpu.VMEM((2080, 128), F32),
            pltpu.VMEM((2080, 128), F32),
            pltpu.VMEM((4, 32, 2048), BF),
            pltpu.VMEM((4, 2048, 32), BF),
            pltpu.VMEM((4, 32, 2048), BF),
            pltpu.VMEM((2080, 128), F32),
            pltpu.VMEM((64, 2048), F32),
        ],
        compiler_params=PARAMS,
    )(ids, counts, *arrived, w)


def home_kernel(ids, counts_sm, back_ref, chosen_ref, out_ref, sorted_ref):
    seg = ids[0]

    def put(t, off):
        tile = back_ref[t].astype(F32)
        sorted_ref[pl.ds(off, 16), :] = tile
        sorted_ref[pl.ds(off + 16, 16), :] = pltpu.roll(tile, 64, 1)
        return off + counts_sm[seg, t]

    in_eights(put, 0)
    rows = jnp.dot(chosen_ref[...], sorted_ref[0:1024, :].astype(BF), preferred_element_type=F32)
    out_ref[...] = rows.T[:64].astype(BF)


def home(ids, counts, back, chosen):
    return pl.pallas_call(
        home_kernel,
        name="home",
        out_shape=jax.ShapeDtypeStruct((64, 1024), BF),
        in_specs=[SM, SM, VM, VM],
        out_specs=VM,
        scratch_shapes=[pltpu.VMEM((1056, 128), F32)],
        compiler_params=PARAMS,
    )(ids, counts, back, chosen)


def last_kernel(ids, mine_ref, h0, h1, h2, h3, wo_ref, out_ref, heads_ref):
    place((h0, h1, h2, h3), ids[1], heads_ref)
    own = jnp.dot(wo_ref[...], heads_ref[...], preferred_element_type=F32)
    out_ref[...] = (mine_ref[...].astype(F32) + own).astype(BF)


def last(ids, mine, heads, wo):
    return pl.pallas_call(
        last_kernel,
        name="last",
        out_shape=jax.ShapeDtypeStruct((64, 1024), BF),
        in_specs=[SM] + [VM] * 6,
        out_specs=VM,
        scratch_shapes=[pltpu.VMEM((256, 1024), BF)],
        compiler_params=PARAMS,
    )(ids, mine, *heads, wo)


def spread(piece):
    def moved(step):
        return lax.ppermute(piece, "ch", [((i + step) % 4, i) for i in range(4)])

    return piece, moved(1), moved(2), moved(3)


def local(
    voxels, neighbours, send_perm, send_counts, conv_weight, qkv_first, out_first, qkv_second, out_second
):
    seg_count = lax.axis_size("seg")
    ids = jnp.stack([lax.axis_index("seg"), lax.axis_index("ch")]).astype(I32)
    up = [(i, i + 1) for i in range(seg_count - 1)]
    down = [(i + 1, i) for i in range(seg_count - 1)]
    prev = lax.ppermute(voxels[-HALO:], "seg", up)
    nxt = lax.ppermute(voxels[:HALO], "seg", down)
    conv_w = jnp.swapaxes(conv_weight, 1, 2)
    w_first = jnp.transpose(qkv_first, (1, 2, 0)).reshape(192, 256)
    w_second = jnp.transpose(qkv_second, (1, 2, 0)).reshape(192, 256)
    own_sum = conv(ids, voxels, neighbours, conv_w)
    mixed_part = edge(ids, prev, nxt, neighbours, conv_w, own_sum)
    mixed_a = spread(mixed_part)
    pick_rows, home_rows, own_out = prep(ids, mixed_part, out_second, send_perm, send_counts)
    heads_a = spread(first(ids, mixed_a, w_first))
    outgoing, mine = pick(ids, mixed_a, heads_a, out_first, pick_rows)
    arrived = lax.all_to_all(outgoing, "seg", split_axis=0, concat_axis=0, tiled=True)
    going = second(ids, send_counts, spread(arrived), w_second)
    back = lax.all_to_all(going, "seg", split_axis=0, concat_axis=0, tiled=True)
    heads_b = spread(home(ids, send_counts, back, home_rows))
    return jnp.swapaxes(last(ids, mine, heads_b, own_out), 0, 1)


def solution(mesh):
    placed = (
        P("seg", None),
        P(None, "seg"),
        P("seg", None),
        P(),
        P(None, None, "ch"),
        P(None, None, "ch"),
        P(),
        P(None, None, "ch"),
        P(),
    )
    return jax.shard_map(
        local, mesh=mesh, in_specs=placed, out_specs=P("seg", "ch"), check_vma=False
    )
```

```python
import jax
import jax.numpy as jnp
import numpy as np
from jax import lax
from jax.experimental import pallas as pl
from jax.experimental.pallas import tpu as pltpu
from jax.sharding import PartitionSpec as P

BF = jnp.bfloat16
F32 = jnp.float32
I32 = jnp.int32
HALO = 128
KOFF = 27
EPS = 1e-05
DEAD = -1e30
EXP_SCALE = float(16 ** (-0.5) * np.log2(np.e))
SAFE_BOUND = float((40.0 * 4) ** 2)
TINY = 1e-30
NT = (((1,), (1,)), ((), ()))
TN = (((0,), (0,)), ((), ()))
DN = lax.GatherDimensionNumbers((), (1,), (1,), (0,), (0,))
VM = pl.BlockSpec(memory_space=pltpu.VMEM)
SM = pl.BlockSpec(memory_space=pltpu.SMEM)
PARAMS = pltpu.CompilerParams(vmem_limit_bytes=50 << 20)


def cost(us):
    return pl.CostEstimate(flops=int(us * 500e6), bytes_accessed=1 << 20, transcendentals=0)


def iota(shape, dim):
    return lax.broadcasted_iota(I32, shape, dim)


def one_where(cond):
    return jnp.where(cond, 1.0, 0.0)


def norm_columns(x):
    centre = x - jnp.mean(x, axis=0, keepdims=True)
    spread = jnp.mean(centre * centre, axis=0, keepdims=True)
    return (centre * lax.rsqrt(spread + EPS)).astype(BF)


def in_eights(step, start):
    def eight(i, carry):
        for j in range(8):
            carry = step(i * 8 + j, carry)
        return carry

    return lax.fori_loop(0, 8, eight, start)


def place(pieces, ch, full_ref):
    size = pieces[0].shape[0]
    for j, piece in enumerate(pieces):
        owner = (ch + j) & 3
        full_ref[pl.ds(pl.multiple_of(owner * size, size), size), :] = piece[...]


def conv_kernel(
    ids, own_hbm, nb_hbm, w_hbm, out_ref, own_ref, nb_ref, w_ref, y_ref, nbs_ref, sems
):
    base = ids[0] * 1024 - HALO
    ch = ids[1]
    pairs = ((nb_hbm, nb_ref), (own_hbm, own_ref), (w_hbm, w_ref))
    copies = [pltpu.make_async_copy(a, b, sems.at[i]) for i, (a, b) in enumerate(pairs)]
    for copy in copies:
        copy.start()
    copies[0].wait()
    for b in range(8):
        nbs_ref[b * 32 : b * 32 + KOFF, :] = nb_ref[:, b * 128 : (b + 1) * 128]
    chosen = one_where(iota((64, 256), 1) == iota((64, 256), 0) + ch * 64).astype(BF)
    copies[1].wait()
    out_ref[...] = lax.dot_general(chosen, own_ref[...], NT, preferred_element_type=F32)
    copies[2].wait()

    def transform(group, slot):
        w = w_ref[pl.ds(group * 3, 3)].reshape(192, 256)
        for j in range(4):
            y_ref[slot, :, j * 256 : (j + 1) * 256] = lax.dot_general(
                w, own_ref[j * 256 : (j + 1) * 256], NT, preferred_element_type=F32
            ).astype(BF)

    def collect(group, slot):
        for kk in range(3):
            collect_one(group * 3 + kk, slot, kk * 64)

    def collect_one(k, slot, top):
        for b in range(8):
            target = nbs_ref[pl.ds(b * 32 + k, 16, stride=0), :]
            r = target - (base + b * 128)
            there = target >= 0
            if b == 0:
                there = there & (r >= 128)
            if b == 7:
                there = there & (r < 256)
            place16 = jnp.where(there, r, 512).astype(jnp.int16)
            lane16 = place16 & jnp.int16(127)
            first = place16 < jnp.int16(128)
            second = place16 < jnp.int16(256)
            third = place16 < jnp.int16(384)
            for g in range(4):
                t = [
                    lax.gather(
                        y_ref[slot, top + g * 16 : top + g * 16 + 16, (b + j - 1) * 128 : (b + j) * 128],
                        lane16[..., None],
                        DN,
                        (1, 1),
                        mode=lax.GatherScatterMode.PROMISE_IN_BOUNDS,
                    )
                    if 0 <= b + j - 1 < 8
                    else None
                    for j in range(3)
                ]
                none = jnp.zeros((16, 128), BF)
                v = none if t[2] is None else jnp.where(third, t[2], none)
                v = jnp.where(second, t[1], v)
                if t[0] is not None:
                    v = jnp.where(first, t[0], v)
                out_ref[g * 16 : g * 16 + 16, b * 128 : (b + 1) * 128] += v.astype(F32)

    transform(0, 0)

    def body(i, carry):
        transform(2 * i + 1, 1)
        collect(2 * i, 0)
        transform(2 * i + 2, 0)
        collect(2 * i + 1, 1)
        return carry

    lax.fori_loop(0, 4, body, 0)
    collect(8, 0)


def conv(ids, own, nb, w):
    stay = [pltpu.with_memory_space_constraint(x, pltpu.HBM) for x in (own, nb, w)]
    return pl.pallas_call(
        conv_kernel,
        name="conv",
        out_shape=jax.ShapeDtypeStruct((64, 1024), F32),
        in_specs=[SM] + [pl.BlockSpec(memory_space=pltpu.HBM)] * 3,
        out_specs=VM,
        scratch_shapes=[
            pltpu.VMEM((1024, 256), BF),
            pltpu.VMEM((KOFF, 1024), I32),
            pltpu.VMEM((KOFF, 64, 256), BF),
            pltpu.VMEM((2, 192, 1024), BF),
            pltpu.VMEM((272, 128), I32),
            pltpu.SemaphoreType.DMA((3,)),
        ],
        compiler_params=PARAMS,
        cost_estimate=cost(8),
    )(ids, *stay)


def edge_kernel(ids, prev_ref, next_ref, nb_ref, w_ref, sum_ref, out_ref, y_ref, acc_ref, nbs_ref):
    base = ids[0] * 1024 - HALO
    for i, b in enumerate((0, 7)):
        nbs_ref[i * 32 : i * 32 + KOFF, :] = nb_ref[:, b * 128 : (b + 1) * 128]
        acc_ref[:, i * 128 : (i + 1) * 128] = sum_ref[:, b * 128 : (b + 1) * 128]
    ends = jnp.concatenate([prev_ref[...], next_ref[...]], 0)
    for i in range(3):
        w = w_ref[i * 9 : (i + 1) * 9].reshape(576, 256)
        y = lax.dot_general(w, ends, NT, preferred_element_type=F32)
        y_ref[i * 9 : (i + 1) * 9] = y.reshape(9, 64, 256)

    def collect(k):
        for i, b in enumerate((0, 7)):
            target = nbs_ref[pl.ds(i * 32 + k, 8, stride=0), :]
            r = target - (base + b * 128)
            there = (target >= 0) & ((r < 128) if b == 0 else (r >= 256))
            lane = r & 127
            for g in range(8):
                at = (slice(g * 8, g * 8 + 8), slice(i * 128, (i + 1) * 128))
                v = jnp.take_along_axis(
                    y_ref[k, at[0], at[1]], lane, axis=1, mode="promise_in_bounds"
                )
                acc_ref[at] += jnp.where(there, v, 0.0)

    def body(i, carry):
        for j in range(3):
            collect(i * 3 + j)
        return carry

    lax.fori_loop(0, 9, body, 0)
    out_ref[:, 128:896] = sum_ref[:, 128:896].astype(BF)
    for i, b in enumerate((0, 7)):
        out_ref[:, b * 128 : (b + 1) * 128] = acc_ref[:, i * 128 : (i + 1) * 128].astype(BF)


def edge(ids, prev, nxt, nb, w, total):
    return pl.pallas_call(
        edge_kernel,
        name="edge",
        out_shape=jax.ShapeDtypeStruct((64, 1024), BF),
        in_specs=[SM] + [VM] * 5,
        out_specs=VM,
        scratch_shapes=[
            pltpu.VMEM((KOFF, 64, 256), F32),
            pltpu.VMEM((64, 256), F32),
            pltpu.VMEM((72, 128), I32),
        ],
        compiler_params=PARAMS,
        cost_estimate=cost(2),
    )(ids, prev, nxt, nb, w, total)


def prep_kernel(ids, after_ref, wo_ref, perm_ref, counts_ref, pick_ref, home_ref, own_ref):
    seg = ids[0]
    ch = ids[1]
    counts = counts_ref[...].astype(F32)
    row = jnp.sum(jnp.where(iota((64, 64), 0) == seg, counts, 0.0), axis=0, keepdims=True)
    slot = iota((512, 64), 0)
    before = jnp.where(iota((512, 64), 1) < (slot >> 3), row, 0.0)
    position = jnp.sum(before, axis=1, keepdims=True).astype(I32)
    position = position + ch * 8 + (iota((512, 1), 0) & 7)
    perm = perm_ref[...].astype(F32)
    hit = iota((512, 1024), 1) == position
    source = jnp.sum(jnp.where(hit, perm, 0.0), axis=1, keepdims=True).astype(I32)
    pick_ref[...] = one_where(iota((512, 1024), 1) == source).astype(BF)
    home_ref[...] = one_where(iota((1024, 1024), 0) == perm_ref[...]).astype(BF)
    chosen = one_where(iota((64, 256), 1) == iota((64, 256), 0) + ch * 64).astype(BF)
    own = lax.dot_general(chosen, wo_ref[...], NT, preferred_element_type=F32)
    own_ref[...] = own.astype(BF)


def prep(ids, after, wo, perm, counts):
    return pl.pallas_call(
        prep_kernel,
        name="prep",
        out_shape=(
            jax.ShapeDtypeStruct((512, 1024), BF),
            jax.ShapeDtypeStruct((1024, 1024), BF),
            jax.ShapeDtypeStruct((64, 256), BF),
        ),
        in_specs=[SM, pl.BlockSpec(memory_space=pl.ANY)] + [VM] * 3,
        out_specs=(VM, VM, VM),
        compiler_params=PARAMS,
        cost_estimate=cost(3),
    )(ids, after, wo, perm, counts)


def stage_heads(qkv, bias, q_ref, k_ref, v_ref):
    rows = qkv.shape[1]
    qkv16 = qkv.astype(BF)
    ones = jnp.ones((16, rows), BF)
    for h in range(4):
        key = qkv16[64 + h * 16 : 80 + h * 16]
        q_ref[h, 0:16, :] = qkv16[h * 16 : (h + 1) * 16]
        if bias is not None:
            key = jnp.concatenate([key, bias], 0)
            q_ref[h, 16:32, :] = ones
        k_ref[h] = key.T
        v_ref[h, 0:16, :] = qkv16[128 + h * 16 : 144 + h * 16]
        v_ref[h, 16:32, :] = ones
    square = qkv16[0:128].astype(F32)
    square = square * square
    longest = [
        jnp.max(jnp.sum(square[i * 16 : (i + 1) * 16], axis=0, keepdims=True)) for i in range(8)
    ]
    bound = longest[0] * longest[4]
    for h in range(1, 4):
        bound = jnp.maximum(bound, longest[h] * longest[4 + h])
    return bound <= SAFE_BOUND


def attend(q_ref, k_ref, v_ref, out_ref, h, keys, cols, shifted):
    s = jnp.dot(k_ref[h, keys, :], q_ref[h, :, cols], preferred_element_type=F32)
    if shifted:
        s = s - jnp.max(s, axis=0, keepdims=True)
    p = jnp.exp2(s * EXP_SCALE).astype(BF)
    o = jnp.dot(v_ref[h, :, keys], p, preferred_element_type=F32)
    o = o[:16] / jnp.maximum(o[16:17], TINY)
    at = h * 16 if isinstance(h, int) else pl.multiple_of(h * 16, 16)
    out_ref[pl.ds(at, 16), cols] = o.astype(out_ref.dtype)


def attend_all(safe, q_ref, k_ref, v_ref, out_ref, patches, block):
    def window(start, size, aligned):
        return pl.ds(start if isinstance(start, int) else pl.multiple_of(start, aligned), size)

    @pl.when(safe)
    def plain():
        def patch(i, carry):
            keys = window(i * 1024, 1024, 1024)
            for qb in range(1024 // block):
                cols = window(i * 1024 + qb * block, block, block)
                for h in range(4):
                    attend(q_ref, k_ref, v_ref, out_ref, h, keys, cols, False)
            return carry

        if patches == 1:
            patch(0, 0)
        else:
            lax.fori_loop(0, patches, patch, 0)

    @pl.when(jnp.logical_not(safe))
    def with_peak():
        def piece(i, carry):
            keys = window((i >> 3) * 1024, 1024, 1024)
            cols = window((i >> 3) * 1024 + (i & 1) * 512, 512, 512)
            attend(q_ref, k_ref, v_ref, out_ref, (i >> 1) & 3, keys, cols, True)
            return carry

        lax.fori_loop(0, patches * 8, piece, 0)


def first_kernel(ids, x0, x1, x2, x3, w_ref, out_ref, full_ref, q_ref, k_ref, v_ref):
    place((x0, x1, x2, x3), ids[1], full_ref)
    normed = norm_columns(full_ref[...].astype(F32))
    qkv = jnp.dot(w_ref[...], normed, preferred_element_type=F32)
    safe = stage_heads(qkv, None, q_ref, k_ref, v_ref)
    attend_all(safe, q_ref, k_ref, v_ref, out_ref, 1, 512)


def first(ids, pieces, w):
    return pl.pallas_call(
        first_kernel,
        name="first",
        out_shape=jax.ShapeDtypeStruct((64, 1024), BF),
        in_specs=[SM] + [VM] * 5,
        out_specs=VM,
        scratch_shapes=[
            pltpu.VMEM((256, 1024), BF),
            pltpu.VMEM((4, 16, 1024), BF),
            pltpu.VMEM((4, 1024, 16), BF),
            pltpu.VMEM((4, 32, 1024), BF),
        ],
        compiler_params=PARAMS,
    )(ids, *pieces, w)


def pick_kernel(ids, x0, x1, x2, x3, h0, h1, h2, h3, wo_ref, chosen_ref, send_ref, mine_ref, full_ref, heads_ref):
    ch = ids[1]
    place((x0, x1, x2, x3), ch, full_ref)
    place((h0, h1, h2, h3), ch, heads_ref)
    mixed = full_ref[...].astype(F32) + lax.dot_general(
        wo_ref[...], heads_ref[...], TN, preferred_element_type=F32
    )
    mixed16 = mixed.astype(BF)
    full_ref[...] = mixed16
    mine_ref[...] = full_ref[pl.ds(pl.multiple_of(ch * 64, 64), 64), :]
    normed = norm_columns(mixed16.astype(F32))
    rows = lax.dot_general(chosen_ref[...], normed, NT, preferred_element_type=F32)
    send_ref[...] = rows.astype(BF).reshape(64, 8, 256)


def pick(ids, mixed, heads, wo, chosen):
    return pl.pallas_call(
        pick_kernel,
        name="pick",
        out_shape=(
            jax.ShapeDtypeStruct((64, 8, 256), BF),
            jax.ShapeDtypeStruct((64, 1024), BF),
        ),
        in_specs=[SM] + [VM] * 10,
        out_specs=(VM, VM),
        scratch_shapes=[pltpu.VMEM((256, 1024), BF), pltpu.VMEM((256, 1024), BF)],
        compiler_params=PARAMS,
        cost_estimate=cost(2),
    )(ids, *mixed, *heads, wo, chosen)


def second_kernel(
    ids, counts_sm, a0, a1, a2, a3, w_ref, out_ref, lo_ref, hi_ref, q_ref, k_ref, v_ref, o_ref, heads_ref
):
    seg = ids[0]
    ch = ids[1]
    lo_ref[...] = jnp.zeros(lo_ref.shape, F32)
    hi_ref[...] = jnp.zeros(hi_ref.shape, F32)

    def compact(s, off):
        tiles = [piece[s].astype(F32) for piece in (a0, a1, a2, a3)]
        for j, tile in enumerate(tiles):
            dst = pl.ds(off + ((ch + j) & 3) * 8, 8)
            lo_ref[dst, :] = tile[:, :128]
            hi_ref[dst, :] = tile[:, 128:]
        return off + counts_sm[s, seg]

    live = in_eights(compact, 0)
    rows = jnp.concatenate([lo_ref[0:2048, :], hi_ref[0:2048, :]], 1).astype(BF)
    qkv = lax.dot_general(w_ref[...], rows, NT, preferred_element_type=F32)
    dead = (iota((16, 2048), 1) >= live) & (iota((16, 2048), 0) == 0)
    bias = jnp.where(dead, DEAD, 0.0).astype(BF)
    safe = stage_heads(qkv, bias, q_ref, k_ref, v_ref)
    o_ref[2048:2080, :] = jnp.zeros((32, 128), F32)

    attend_all(safe, q_ref, k_ref, v_ref, heads_ref, 2, 1024)
    for i in range(2):
        rows = slice(i * 1024, (i + 1) * 1024)
        o = heads_ref[:, rows]
        o_ref[rows, :] = jnp.concatenate([o, o], 0).T
    low = iota((16, 128), 1) < 64

    def give(s, off):
        top = o_ref[pl.ds(off, 16), :]
        end = o_ref[pl.ds(off + 16, 16), :]
        out_ref[s] = jnp.where(low, top, end).astype(BF)
        return off + counts_sm[s, seg]

    in_eights(give, 0)


def second(ids, counts, arrived, w):
    return pl.pallas_call(
        second_kernel,
        name="second",
        out_shape=jax.ShapeDtypeStruct((64, 16, 128), BF),
        in_specs=[SM, SM] + [VM] * 5,
        out_specs=VM,
        scratch_shapes=[
            pltpu.VMEM((2080, 128), F32),
            pltpu.VMEM((2080, 128), F32),
            pltpu.VMEM((4, 32, 2048), BF),
            pltpu.VMEM((4, 2048, 32), BF),
            pltpu.VMEM((4, 32, 2048), BF),
            pltpu.VMEM((2080, 128), F32),
            pltpu.VMEM((64, 2048), F32),
        ],
        compiler_params=PARAMS,
    )(ids, counts, *arrived, w)


def home_kernel(ids, counts_sm, back_ref, chosen_ref, out_ref, sorted_ref):
    seg = ids[0]

    def put(t, off):
        tile = back_ref[t].astype(F32)
        sorted_ref[pl.ds(off, 16), :] = tile
        sorted_ref[pl.ds(off + 16, 16), :] = pltpu.roll(tile, 64, 1)
        return off + counts_sm[seg, t]

    in_eights(put, 0)
    rows = jnp.dot(chosen_ref[...], sorted_ref[0:1024, :].astype(BF), preferred_element_type=F32)
    out_ref[...] = rows.T[:64].astype(BF)


def home(ids, counts, back, chosen):
    return pl.pallas_call(
        home_kernel,
        name="home",
        out_shape=jax.ShapeDtypeStruct((64, 1024), BF),
        in_specs=[SM, SM, VM, VM],
        out_specs=VM,
        scratch_shapes=[pltpu.VMEM((1056, 128), F32)],
        compiler_params=PARAMS,
    )(ids, counts, back, chosen)


def last_kernel(ids, mine_ref, h0, h1, h2, h3, wo_ref, out_ref, heads_ref):
    place((h0, h1, h2, h3), ids[1], heads_ref)
    own = jnp.dot(wo_ref[...], heads_ref[...], preferred_element_type=F32)
    out_ref[...] = (mine_ref[...].astype(F32) + own).astype(BF)


def last(ids, mine, heads, wo):
    return pl.pallas_call(
        last_kernel,
        name="last",
        out_shape=jax.ShapeDtypeStruct((64, 1024), BF),
        in_specs=[SM] + [VM] * 6,
        out_specs=VM,
        scratch_shapes=[pltpu.VMEM((256, 1024), BF)],
        compiler_params=PARAMS,
    )(ids, mine, *heads, wo)


def spread(piece):
    def moved(step):
        return lax.ppermute(piece, "ch", [((i + step) % 4, i) for i in range(4)])

    return piece, moved(1), moved(2), moved(3)


def local(
    voxels, neighbours, send_perm, send_counts, conv_weight, qkv_first, out_first, qkv_second, out_second
):
    seg_count = lax.axis_size("seg")
    ids = jnp.stack([lax.axis_index("seg"), lax.axis_index("ch")]).astype(I32)
    up = [(i, i + 1) for i in range(seg_count - 1)]
    down = [(i + 1, i) for i in range(seg_count - 1)]
    prev = lax.ppermute(voxels[-HALO:], "seg", up)
    nxt = lax.ppermute(voxels[:HALO], "seg", down)
    conv_w = jnp.swapaxes(conv_weight, 1, 2)
    w_first = jnp.transpose(qkv_first, (1, 2, 0)).reshape(192, 256)
    w_second = jnp.transpose(qkv_second, (1, 2, 0)).reshape(192, 256)
    own_sum = conv(ids, voxels, neighbours, conv_w)
    mixed_part = edge(ids, prev, nxt, neighbours, conv_w, own_sum)
    mixed_a = spread(mixed_part)
    pick_rows, home_rows, own_out = prep(ids, mixed_part, out_second, send_perm, send_counts)
    heads_a = spread(first(ids, mixed_a, w_first))
    outgoing, mine = pick(ids, mixed_a, heads_a, out_first, pick_rows)
    arrived = lax.all_to_all(outgoing, "seg", split_axis=0, concat_axis=0, tiled=True)
    going = second(ids, send_counts, spread(arrived), w_second)
    back = lax.all_to_all(going, "seg", split_axis=0, concat_axis=0, tiled=True)
    heads_b = spread(home(ids, send_counts, back, home_rows))
    return jnp.swapaxes(last(ids, mine, heads_b, own_out), 0, 1)


def solution(mesh):
    placed = (
        P("seg", None),
        P(None, "seg"),
        P("seg", None),
        P(),
        P(None, None, "ch"),
        P(None, None, "ch"),
        P(),
        P(None, None, "ch"),
        P(),
    )
    return jax.shard_map(
        local, mesh=mesh, in_specs=placed, out_specs=P("seg", "ch"), check_vma=False
    )
```

```python
import jax
import jax.numpy as jnp
import numpy as np
from jax import lax
from jax.experimental import pallas as pl
from jax.experimental.pallas import tpu as pltpu
from jax.sharding import PartitionSpec as P

BF = jnp.bfloat16
F32 = jnp.float32
I32 = jnp.int32
HALO = 128
KOFF = 27
EPS = 1e-05
DEAD = -1e30
EXP_SCALE = float(16 ** (-0.5) * np.log2(np.e))
SAFE_BOUND = float((40.0 * 4) ** 2)
TINY = 1e-30
NT = (((1,), (1,)), ((), ()))
TN = (((0,), (0,)), ((), ()))
DN = lax.GatherDimensionNumbers((), (1,), (1,), (0,), (0,))
STEPS = (0, 1, 3, 2)
VM = pl.BlockSpec(memory_space=pltpu.VMEM)
SM = pl.BlockSpec(memory_space=pltpu.SMEM)
PARAMS = pltpu.CompilerParams(vmem_limit_bytes=50 << 20)


def cost(us):
    return pl.CostEstimate(flops=int(us * 500e6), bytes_accessed=1 << 20, transcendentals=0)


def iota(shape, dim):
    return lax.broadcasted_iota(I32, shape, dim)


def one_where(cond):
    return jnp.where(cond, 1.0, 0.0)


def norm_columns(x):
    centre = x - jnp.mean(x, axis=0, keepdims=True)
    spread = jnp.mean(centre * centre, axis=0, keepdims=True)
    return (centre * lax.rsqrt(spread + EPS)).astype(BF)


def in_eights(step, start):
    def eight(i, carry):
        for j in range(8):
            carry = step(i * 8 + j, carry)
        return carry

    return lax.fori_loop(0, 8, eight, start)


def place(pieces, ch, full_ref):
    size = pieces[0].shape[0]
    for j, piece in zip(STEPS, pieces):
        owner = (ch + j) & 3
        full_ref[pl.ds(pl.multiple_of(owner * size, size), size), :] = piece[...]


def conv_kernel(
    ids, own_hbm, nb_hbm, w_hbm, out_ref, own_ref, nb_ref, w_ref, y_ref, nbs_ref, sems
):
    base = ids[0] * 1024 - HALO
    ch = ids[1]
    pairs = ((nb_hbm, nb_ref), (own_hbm, own_ref), (w_hbm, w_ref))
    copies = [pltpu.make_async_copy(a, b, sems.at[i]) for i, (a, b) in enumerate(pairs)]
    for copy in copies:
        copy.start()
    copies[0].wait()
    for b in range(8):
        nbs_ref[b * 32 : b * 32 + KOFF, :] = nb_ref[:, b * 128 : (b + 1) * 128]
    chosen = one_where(iota((64, 256), 1) == iota((64, 256), 0) + ch * 64).astype(BF)
    copies[1].wait()
    out_ref[...] = lax.dot_general(chosen, own_ref[...], NT, preferred_element_type=F32)
    copies[2].wait()

    def transform(group, slot):
        w = w_ref[pl.ds(group * 3, 3)].reshape(192, 256)
        for j in range(4):
            y_ref[slot, :, j * 256 : (j + 1) * 256] = lax.dot_general(
                w, own_ref[j * 256 : (j + 1) * 256], NT, preferred_element_type=F32
            ).astype(BF)

    def collect(group, slot):
        for kk in range(3):
            collect_one(group * 3 + kk, slot, kk * 64)

    def collect_one(k, slot, top):
        for b in range(8):
            target = nbs_ref[pl.ds(b * 32 + k, 16, stride=0), :]
            r = target - (base + b * 128)
            there = target >= 0
            if b == 0:
                there = there & (r >= 128)
            if b == 7:
                there = there & (r < 256)
            place16 = jnp.where(there, r, 512).astype(jnp.int16)
            lane16 = place16 & jnp.int16(127)
            first = place16 < jnp.int16(128)
            second = place16 < jnp.int16(256)
            third = place16 < jnp.int16(384)
            for g in range(4):
                t = [
                    lax.gather(
                        y_ref[slot, top + g * 16 : top + g * 16 + 16, (b + j - 1) * 128 : (b + j) * 128],
                        lane16[..., None],
                        DN,
                        (1, 1),
                        mode=lax.GatherScatterMode.PROMISE_IN_BOUNDS,
                    )
                    if 0 <= b + j - 1 < 8
                    else None
                    for j in range(3)
                ]
                none = jnp.zeros((16, 128), BF)
                v = none if t[2] is None else jnp.where(third, t[2], none)
                v = jnp.where(second, t[1], v)
                if t[0] is not None:
                    v = jnp.where(first, t[0], v)
                out_ref[g * 16 : g * 16 + 16, b * 128 : (b + 1) * 128] += v.astype(F32)

    transform(0, 0)

    def body(i, carry):
        transform(2 * i + 1, 1)
        collect(2 * i, 0)
        transform(2 * i + 2, 0)
        collect(2 * i + 1, 1)
        return carry

    lax.fori_loop(0, 4, body, 0)
    collect(8, 0)


def conv(ids, own, nb, w):
    stay = [pltpu.with_memory_space_constraint(x, pltpu.HBM) for x in (own, nb, w)]
    return pl.pallas_call(
        conv_kernel,
        name="conv",
        out_shape=jax.ShapeDtypeStruct((64, 1024), F32),
        in_specs=[SM] + [pl.BlockSpec(memory_space=pltpu.HBM)] * 3,
        out_specs=VM,
        scratch_shapes=[
            pltpu.VMEM((1024, 256), BF),
            pltpu.VMEM((KOFF, 1024), I32),
            pltpu.VMEM((KOFF, 64, 256), BF),
            pltpu.VMEM((2, 192, 1024), BF),
            pltpu.VMEM((272, 128), I32),
            pltpu.SemaphoreType.DMA((3,)),
        ],
        compiler_params=PARAMS,
        cost_estimate=cost(8),
    )(ids, *stay)


def edge_kernel(ids, prev_ref, next_ref, nb_ref, w_ref, sum_ref, out_ref, y_ref, acc_ref, nbs_ref):
    base = ids[0] * 1024 - HALO
    for i, b in enumerate((0, 7)):
        nbs_ref[i * 32 : i * 32 + KOFF, :] = nb_ref[:, b * 128 : (b + 1) * 128]
        acc_ref[:, i * 128 : (i + 1) * 128] = sum_ref[:, b * 128 : (b + 1) * 128]
    ends = jnp.concatenate([prev_ref[...], next_ref[...]], 0)
    for i in range(3):
        w = w_ref[i * 9 : (i + 1) * 9].reshape(576, 256)
        y = lax.dot_general(w, ends, NT, preferred_element_type=F32)
        y_ref[i * 9 : (i + 1) * 9] = y.reshape(9, 64, 256)

    def collect(k):
        for i, b in enumerate((0, 7)):
            target = nbs_ref[pl.ds(i * 32 + k, 8, stride=0), :]
            r = target - (base + b * 128)
            there = (target >= 0) & ((r < 128) if b == 0 else (r >= 256))
            lane = r & 127
            for g in range(8):
                at = (slice(g * 8, g * 8 + 8), slice(i * 128, (i + 1) * 128))
                v = jnp.take_along_axis(
                    y_ref[k, at[0], at[1]], lane, axis=1, mode="promise_in_bounds"
                )
                acc_ref[at] += jnp.where(there, v, 0.0)

    def body(i, carry):
        for j in range(3):
            collect(i * 3 + j)
        return carry

    lax.fori_loop(0, 9, body, 0)
    out_ref[:, 128:896] = sum_ref[:, 128:896].astype(BF)
    for i, b in enumerate((0, 7)):
        out_ref[:, b * 128 : (b + 1) * 128] = acc_ref[:, i * 128 : (i + 1) * 128].astype(BF)


def edge(ids, prev, nxt, nb, w, total):
    return pl.pallas_call(
        edge_kernel,
        name="edge",
        out_shape=jax.ShapeDtypeStruct((64, 1024), BF),
        in_specs=[SM] + [VM] * 5,
        out_specs=VM,
        scratch_shapes=[
            pltpu.VMEM((KOFF, 64, 256), F32),
            pltpu.VMEM((64, 256), F32),
            pltpu.VMEM((72, 128), I32),
        ],
        compiler_params=PARAMS,
        cost_estimate=cost(2),
    )(ids, prev, nxt, nb, w, total)


def prep_kernel(ids, after_ref, wo_ref, perm_ref, counts_ref, pick_ref, home_ref, own_ref):
    seg = ids[0]
    ch = ids[1]
    counts = counts_ref[...].astype(F32)
    row = jnp.sum(jnp.where(iota((64, 64), 0) == seg, counts, 0.0), axis=0, keepdims=True)
    slot = iota((512, 64), 0)
    before = jnp.where(iota((512, 64), 1) < (slot >> 3), row, 0.0)
    position = jnp.sum(before, axis=1, keepdims=True).astype(I32)
    position = position + ch * 8 + (iota((512, 1), 0) & 7)
    perm = perm_ref[...].astype(F32)
    hit = iota((512, 1024), 1) == position
    source = jnp.sum(jnp.where(hit, perm, 0.0), axis=1, keepdims=True).astype(I32)
    pick_ref[...] = one_where(iota((512, 1024), 1) == source).astype(BF)
    home_ref[...] = one_where(iota((1024, 1024), 0) == perm_ref[...]).astype(BF)
    chosen = one_where(iota((64, 256), 1) == iota((64, 256), 0) + ch * 64).astype(BF)
    own = lax.dot_general(chosen, wo_ref[...], NT, preferred_element_type=F32)
    own_ref[...] = own.astype(BF)


def prep(ids, after, wo, perm, counts):
    return pl.pallas_call(
        prep_kernel,
        name="prep",
        out_shape=(
            jax.ShapeDtypeStruct((512, 1024), BF),
            jax.ShapeDtypeStruct((1024, 1024), BF),
            jax.ShapeDtypeStruct((64, 256), BF),
        ),
        in_specs=[SM, pl.BlockSpec(memory_space=pl.ANY)] + [VM] * 3,
        out_specs=(VM, VM, VM),
        compiler_params=PARAMS,
        cost_estimate=cost(3),
    )(ids, after, wo, perm, counts)


def stage_heads(qkv, bias, q_ref, k_ref, v_ref):
    rows = qkv.shape[1]
    qkv16 = qkv.astype(BF)
    ones = jnp.ones((16, rows), BF)
    for h in range(4):
        key = qkv16[64 + h * 16 : 80 + h * 16]
        q_ref[h, 0:16, :] = qkv16[h * 16 : (h + 1) * 16]
        if bias is not None:
            key = jnp.concatenate([key, bias], 0)
            q_ref[h, 16:32, :] = ones
        k_ref[h] = key.T
        v_ref[h, 0:16, :] = qkv16[128 + h * 16 : 144 + h * 16]
        v_ref[h, 16:32, :] = ones
    square = qkv16[0:128].astype(F32)
    square = square * square
    longest = [
        jnp.max(jnp.sum(square[i * 16 : (i + 1) * 16], axis=0, keepdims=True)) for i in range(8)
    ]
    bound = longest[0] * longest[4]
    for h in range(1, 4):
        bound = jnp.maximum(bound, longest[h] * longest[4 + h])
    return bound <= SAFE_BOUND


def attend(q_ref, k_ref, v_ref, out_ref, h, keys, cols, shifted):
    s = jnp.dot(k_ref[h, keys, :], q_ref[h, :, cols], preferred_element_type=F32)
    if shifted:
        s = s - jnp.max(s, axis=0, keepdims=True)
    p = jnp.exp2(s * EXP_SCALE).astype(BF)
    o = jnp.dot(v_ref[h, :, keys], p, preferred_element_type=F32)
    o = o[:16] / jnp.maximum(o[16:17], TINY)
    at = h * 16 if isinstance(h, int) else pl.multiple_of(h * 16, 16)
    out_ref[pl.ds(at, 16), cols] = o.astype(out_ref.dtype)


def attend_all(safe, q_ref, k_ref, v_ref, out_ref, patches, block):
    def window(start, size, aligned):
        return pl.ds(start if isinstance(start, int) else pl.multiple_of(start, aligned), size)

    @pl.when(safe)
    def plain():
        def patch(i, carry):
            keys = window(i * 1024, 1024, 1024)
            for qb in range(1024 // block):
                cols = window(i * 1024 + qb * block, block, block)
                for h in range(4):
                    attend(q_ref, k_ref, v_ref, out_ref, h, keys, cols, False)
            return carry

        if patches == 1:
            patch(0, 0)
        else:
            lax.fori_loop(0, patches, patch, 0)

    @pl.when(jnp.logical_not(safe))
    def with_peak():
        def piece(i, carry):
            keys = window((i >> 3) * 1024, 1024, 1024)
            cols = window((i >> 3) * 1024 + (i & 1) * 512, 512, 512)
            attend(q_ref, k_ref, v_ref, out_ref, (i >> 1) & 3, keys, cols, True)
            return carry

        lax.fori_loop(0, patches * 8, piece, 0)


def first_kernel(ids, x0, x1, x2, x3, w_ref, out_ref, full_ref, q_ref, k_ref, v_ref):
    place((x0, x1, x2, x3), ids[1], full_ref)
    normed = norm_columns(full_ref[...].astype(F32))
    qkv = jnp.dot(w_ref[...], normed, preferred_element_type=F32)
    safe = stage_heads(qkv, None, q_ref, k_ref, v_ref)
    attend_all(safe, q_ref, k_ref, v_ref, out_ref, 1, 512)


def first(ids, pieces, w):
    return pl.pallas_call(
        first_kernel,
        name="first",
        out_shape=jax.ShapeDtypeStruct((64, 1024), BF),
        in_specs=[SM] + [VM] * 5,
        out_specs=VM,
        scratch_shapes=[
            pltpu.VMEM((256, 1024), BF),
            pltpu.VMEM((4, 16, 1024), BF),
            pltpu.VMEM((4, 1024, 16), BF),
            pltpu.VMEM((4, 32, 1024), BF),
        ],
        compiler_params=PARAMS,
    )(ids, *pieces, w)


def pick_kernel(ids, x0, x1, x2, x3, h0, h1, h2, h3, wo_ref, chosen_ref, send_ref, mine_ref, full_ref, heads_ref):
    ch = ids[1]
    place((x0, x1, x2, x3), ch, full_ref)
    place((h0, h1, h2, h3), ch, heads_ref)
    mixed = full_ref[...].astype(F32) + lax.dot_general(
        wo_ref[...], heads_ref[...], TN, preferred_element_type=F32
    )
    mixed16 = mixed.astype(BF)
    full_ref[...] = mixed16
    mine_ref[...] = full_ref[pl.ds(pl.multiple_of(ch * 64, 64), 64), :]
    normed = norm_columns(mixed16.astype(F32))
    rows = lax.dot_general(chosen_ref[...], normed, NT, preferred_element_type=F32)
    send_ref[...] = rows.astype(BF).reshape(64, 8, 256)


def pick(ids, mixed, heads, wo, chosen):
    return pl.pallas_call(
        pick_kernel,
        name="pick",
        out_shape=(
            jax.ShapeDtypeStruct((64, 8, 256), BF),
            jax.ShapeDtypeStruct((64, 1024), BF),
        ),
        in_specs=[SM] + [VM] * 10,
        out_specs=(VM, VM),
        scratch_shapes=[pltpu.VMEM((256, 1024), BF), pltpu.VMEM((256, 1024), BF)],
        compiler_params=PARAMS,
        cost_estimate=cost(2),
    )(ids, *mixed, *heads, wo, chosen)


def second_kernel(
    ids, counts_sm, a0, a1, a2, a3, w_ref, out_ref, lo_ref, hi_ref, q_ref, k_ref, v_ref, o_ref, heads_ref
):
    seg = ids[0]
    ch = ids[1]
    lo_ref[...] = jnp.zeros(lo_ref.shape, F32)
    hi_ref[...] = jnp.zeros(hi_ref.shape, F32)

    def compact(s, off):
        tiles = [piece[s].astype(F32) for piece in (a0, a1, a2, a3)]
        for j, tile in zip(STEPS, tiles):
            dst = pl.ds(off + ((ch + j) & 3) * 8, 8)
            lo_ref[dst, :] = tile[:, :128]
            hi_ref[dst, :] = tile[:, 128:]
        return off + counts_sm[s, seg]

    live = in_eights(compact, 0)
    rows = jnp.concatenate([lo_ref[0:2048, :], hi_ref[0:2048, :]], 1).astype(BF)
    qkv = lax.dot_general(w_ref[...], rows, NT, preferred_element_type=F32)
    dead = (iota((16, 2048), 1) >= live) & (iota((16, 2048), 0) == 0)
    bias = jnp.where(dead, DEAD, 0.0).astype(BF)
    safe = stage_heads(qkv, bias, q_ref, k_ref, v_ref)
    o_ref[2048:2080, :] = jnp.zeros((32, 128), F32)

    attend_all(safe, q_ref, k_ref, v_ref, heads_ref, 2, 1024)
    for i in range(2):
        rows = slice(i * 1024, (i + 1) * 1024)
        o = heads_ref[:, rows]
        o_ref[rows, :] = jnp.concatenate([o, o], 0).T
    low = iota((16, 128), 1) < 64

    def give(s, off):
        top = o_ref[pl.ds(off, 16), :]
        end = o_ref[pl.ds(off + 16, 16), :]
        out_ref[s] = jnp.where(low, top, end).astype(BF)
        return off + counts_sm[s, seg]

    in_eights(give, 0)


def second(ids, counts, arrived, w):
    return pl.pallas_call(
        second_kernel,
        name="second",
        out_shape=jax.ShapeDtypeStruct((64, 16, 128), BF),
        in_specs=[SM, SM] + [VM] * 5,
        out_specs=VM,
        scratch_shapes=[
            pltpu.VMEM((2080, 128), F32),
            pltpu.VMEM((2080, 128), F32),
            pltpu.VMEM((4, 32, 2048), BF),
            pltpu.VMEM((4, 2048, 32), BF),
            pltpu.VMEM((4, 32, 2048), BF),
            pltpu.VMEM((2080, 128), F32),
            pltpu.VMEM((64, 2048), F32),
        ],
        compiler_params=PARAMS,
    )(ids, counts, *arrived, w)


def home_kernel(ids, counts_sm, back_ref, chosen_ref, out_ref, sorted_ref):
    seg = ids[0]

    def put(t, off):
        tile = back_ref[t].astype(F32)
        sorted_ref[pl.ds(off, 16), :] = tile
        sorted_ref[pl.ds(off + 16, 16), :] = pltpu.roll(tile, 64, 1)
        return off + counts_sm[seg, t]

    in_eights(put, 0)
    rows = jnp.dot(chosen_ref[...], sorted_ref[0:1024, :].astype(BF), preferred_element_type=F32)
    out_ref[...] = rows.T[:64].astype(BF)


def home(ids, counts, back, chosen):
    return pl.pallas_call(
        home_kernel,
        name="home",
        out_shape=jax.ShapeDtypeStruct((64, 1024), BF),
        in_specs=[SM, SM, VM, VM],
        out_specs=VM,
        scratch_shapes=[pltpu.VMEM((1056, 128), F32)],
        compiler_params=PARAMS,
    )(ids, counts, back, chosen)


def last_kernel(ids, mine_ref, h0, h1, h2, h3, wo_ref, out_ref, heads_ref):
    place((h0, h1, h2, h3), ids[1], heads_ref)
    own = jnp.dot(wo_ref[...], heads_ref[...], preferred_element_type=F32)
    out_ref[...] = (mine_ref[...].astype(F32) + own).astype(BF)


def last(ids, mine, heads, wo):
    return pl.pallas_call(
        last_kernel,
        name="last",
        out_shape=jax.ShapeDtypeStruct((64, 1024), BF),
        in_specs=[SM] + [VM] * 6,
        out_specs=VM,
        scratch_shapes=[pltpu.VMEM((256, 1024), BF)],
        compiler_params=PARAMS,
    )(ids, mine, *heads, wo)


def spread(piece):
    def moved(step):
        return lax.ppermute(piece, "ch", [((i + step) % 4, i) for i in range(4)])

    return piece, moved(1), moved(3), moved(2)


def local(
    voxels, neighbours, send_perm, send_counts, conv_weight, qkv_first, out_first, qkv_second, out_second
):
    seg_count = lax.axis_size("seg")
    ids = jnp.stack([lax.axis_index("seg"), lax.axis_index("ch")]).astype(I32)
    up = [(i, i + 1) for i in range(seg_count - 1)]
    down = [(i + 1, i) for i in range(seg_count - 1)]
    prev = lax.ppermute(voxels[-HALO:], "seg", up)
    nxt = lax.ppermute(voxels[:HALO], "seg", down)
    conv_w = jnp.swapaxes(conv_weight, 1, 2)
    w_first = jnp.transpose(qkv_first, (1, 2, 0)).reshape(192, 256)
    w_second = jnp.transpose(qkv_second, (1, 2, 0)).reshape(192, 256)
    own_sum = conv(ids, voxels, neighbours, conv_w)
    mixed_part = edge(ids, prev, nxt, neighbours, conv_w, own_sum)
    mixed_a = spread(mixed_part)
    pick_rows, home_rows, own_out = prep(ids, mixed_part, out_second, send_perm, send_counts)
    heads_a = spread(first(ids, mixed_a, w_first))
    outgoing, mine = pick(ids, mixed_a, heads_a, out_first, pick_rows)
    arrived = lax.all_to_all(outgoing, "seg", split_axis=0, concat_axis=0, tiled=True)
    going = second(ids, send_counts, spread(arrived), w_second)
    back = lax.all_to_all(going, "seg", split_axis=0, concat_axis=0, tiled=True)
    heads_b = spread(home(ids, send_counts, back, home_rows))
    return jnp.swapaxes(last(ids, mine, heads_b, own_out), 0, 1)


def solution(mesh):
    placed = (
        P("seg", None),
        P(None, "seg"),
        P("seg", None),
        P(),
        P(None, None, "ch"),
        P(None, None, "ch"),
        P(),
        P(None, None, "ch"),
        P(),
    )
    return jax.shard_map(
        local, mesh=mesh, in_specs=placed, out_specs=P("seg", "ch"), check_vma=False
    )
```
